32 devices in a mesh: seq: 16 (over z, y, x), head: 2 (over core).
Axes of the slice: x: 2, y: 2, z: 4, core: 2. Of those that a mesh axis runs over, the one named last changes fastest.
Arguments:
- query_raw: bfloat16 [2048, 2048], P('seq', 'head'), may hold values from -6 to 6
- key_raw: bfloat16 [2048, 2048], P('seq', 'head'), may hold values from -6 to 6
- value_raw: bfloat16 [2048, 2048], P('seq', 'head'), may hold values from -6 to 6
- gate_raw: float32 [2048, 2048], P('seq', 'head')
- beta_raw: float32 [2048, 16], P('seq', 'head'), may hold values from -8.5 to 3.5
- conv_weight: float32 [3, 4, 2048], P(None, None, 'head'), may hold values from -3 to 3
- decay_log: float32 [2048], P('head')
- grad_out: bfloat16 [2048, 2048], P('seq', 'head'), may hold values from -6 to 6
Outputs:
- query_grad: bfloat16 [2048, 2048], P('seq', 'head')
- key_grad: bfloat16 [2048, 2048], P('seq', 'head')
- value_grad: bfloat16 [2048, 2048], P('seq', 'head')
- gate_grad: float32 [2048, 2048], P('seq', 'head')
- beta_grad: float32 [2048, 16], P('seq', 'head')
- conv_grad: float32 [3, 4, 2048], P(None, None, 'head')
- decay_grad: float32 [2048], P('head')
The draws below stay inside these ranges and needn't reach their ends.
All inputs are finite; a program needn't handle non-finite values.
Results may differ from the reference program's by a relative error of at most 0.0018.
Values may be sent and summed in bfloat16 or wider, within the bound.
A program may use at most 128 MiB of HBM per device.

```python
import jax
import jax.numpy as jnp
from jax import lax

HEADS = 16
DK = 128
KCONV = 4
TOK_DEV = 128
TOKENS = 2048
CH = 2048


def gate_parts(key):
    base = jax.random.fold_in(key, 7)
    pick_key, fast_key, slow_key, normal_key, spot_key, loss_key = jax.random.split(base, 6)
    channels = HEADS * DK
    share = 0.5
    slow = jax.random.uniform(pick_key, (channels,)) < share
    fast_speed = jnp.exp(jax.random.uniform(fast_key, (channels,), minval=jnp.log(1.0 / 50.0), maxval=jnp.log(1.0 / 30.0)))
    slow_speed = jnp.log(10.0) / TOKENS * jnp.exp(jax.random.uniform(slow_key, (channels,), minval=jnp.log(0.02), maxval=jnp.log(0.2)))
    speed = jnp.where(slow, slow_speed, fast_speed)
    decay_values = jnp.log(speed / 0.8)
    score_logits = jnp.clip(jax.random.normal(normal_key, (TOKENS, channels)), -3.0, 3.0)
    spots = jax.random.randint(spot_key, (3,), 0, TOKENS)
    losses = jax.random.uniform(loss_key, (channels,), minval=0.22, maxval=0.5)
    target_value = losses / (speed / 0.8)
    spike_amount = target_value + jnp.log(-jnp.expm1(-target_value))
    positions = jnp.arange(TOKENS)
    flagged_entries = jnp.any(positions[:, None] == spots[None, :], axis=1)
    score_logits = jnp.where(flagged_entries[:, None], spike_amount[None, :], score_logits)
    return (decay_values.astype(jnp.float32), score_logits.astype(jnp.float32))


def draw_decay_log(key, part):
    return gate_parts(key)[0]


def draw_gate_raw(key, part):
    return gate_parts(key)[1]


def draw_beta_raw(key, part):
    center_key, noise_key = jax.random.split(jax.random.fold_in(key, 3))
    centers = jax.random.uniform(center_key, (HEADS,), minval=-6.0, maxval=1.0)
    noise = jnp.clip(jax.random.normal(noise_key, (TOKENS, HEADS)), -2.5, 2.5) * 0.8
    return (centers[None, :] + noise).astype(jnp.float32)


def block_scale(rng, dims, cuts, low, largest):
    def one(axis_at, parts):
        heights = jax.random.uniform(jax.random.fold_in(jax.random.fold_in(rng, 6), axis_at), (parts,), jnp.float32, low / len(cuts), largest / len(cuts))
        return jnp.repeat(jnp.exp(heights), dims[axis_at] // parts).reshape((-1,) + (1,) * (len(dims) - axis_at - 1))

    loudness = one(*cuts[0])
    for cut in cuts[1:]:
        loudness = loudness * one(*cut)
    return loudness


def centred(rng, dims, deviation, limit, shards=(), held_as=jnp.bfloat16):
    result = jax.random.normal(rng, dims, jnp.float32) * deviation
    if len(shards) > 0:
        result = block_scale(rng, dims, shards, -0.22, 0.18) * result
    return jnp.clip(result, min=-limit, max=limit).astype(held_as)


def setup_inputs(seed: int = 0) -> dict:
    arg_keys = jax.random.split(jax.random.key(seed), 9)
    return {
        "query_raw": centred(arg_keys[0], (TOKENS, CH), 1.0, 6.0, ((0, 16), (1, 2))),
        "key_raw": centred(arg_keys[1], (TOKENS, CH), 1.0, 6.0, ((0, 16), (1, 2))),
        "value_raw": centred(arg_keys[2], (TOKENS, CH), 1.0, 6.0, ((0, 16), (1, 2))),
        "gate_raw": draw_gate_raw(jax.random.fold_in(arg_keys[8], 71), 0),
        "beta_raw": draw_beta_raw(jax.random.fold_in(arg_keys[8], 71), 0),
        "conv_weight": centred(arg_keys[5], (3, KCONV, CH), KCONV ** -0.5, 3.0, ((2, 2),), jnp.float32),
        "decay_log": draw_decay_log(jax.random.fold_in(arg_keys[8], 71), 0),
        "grad_out": centred(arg_keys[7], (TOKENS, CH), 1.0, 6.0, ((0, 16), (1, 2))),
    }


largest_entry = lax.Precision.HIGHEST
epsilon = 1e-06

def conv_silu(source, weights):
    margin = weights.shape[0] - 1
    length = source.shape[0]
    padded = jnp.concatenate([jnp.zeros((margin, source.shape[1]), jnp.float32), source], 0)
    summed = weights[0] * padded[0:length]
    for offset in range(1, weights.shape[0]):
        summed = summed + weights[offset] * padded[offset:offset + length]
    return jax.nn.silu(summed)

def unit_heads(vectors):
    return vectors * lax.rsqrt(lax.optimization_barrier(jnp.sum(vectors * vectors, axis=-1, keepdims=True)) + epsilon)

def layer_outputs(query_in, key_in, value_in, gate_in, beta_in, conv_in, decay_in):
    length = gate_in.shape[0]
    head_count = beta_in.shape[1]
    head_width = gate_in.shape[1] // head_count
    head_shape = (length, head_count, head_width)
    queries = unit_heads(conv_silu(query_in, conv_in[0]).reshape(head_shape))
    keys = unit_heads(conv_silu(key_in, conv_in[1]).reshape(head_shape))
    values = conv_silu(value_in, conv_in[2]).reshape(head_shape)
    log_decay = (-jnp.exp(decay_in) * jax.nn.softplus(gate_in)).reshape(head_shape)
    beta_rate = jax.nn.sigmoid(beta_in)
    block_count = length // TOK_DEV

    def token_step(recall_memory, sliced):
        single_query_row, single_key_row, value_row, decay_row, beta_row = sliced
        recall_memory = recall_memory * jnp.exp(decay_row)[:, :, None]
        predicted_value = jnp.einsum('pjf,pj->pf', recall_memory, single_key_row, precision=largest_entry)
        recall_memory = recall_memory + beta_row[:, None, None] * single_key_row[:, :, None] * (value_row - predicted_value)[:, None, :]
        return (recall_memory, jnp.einsum('pjf,pj->pf', recall_memory, single_query_row, precision=largest_entry))

    def block_step(recall_memory, sliced):
        return lax.scan(token_step, recall_memory, sliced)
    blocked = tuple((array.reshape((block_count, TOK_DEV) + array.shape[1:]) for array in (queries, keys, values, log_decay, beta_rate)))
    initial = jnp.zeros((head_count, head_width, head_width), jnp.float32)
    unused, outputs = lax.scan(jax.checkpoint(block_step), initial, blocked)
    return outputs.reshape(length, head_count * head_width)

def reference(query_raw, key_raw, value_raw, gate_raw, beta_raw, conv_weight, decay_log, grad_out):
    primal, pullback = jax.vjp(layer_outputs, query_raw.astype(jnp.float32), key_raw.astype(jnp.float32), value_raw.astype(jnp.float32), gate_raw, beta_raw, conv_weight, decay_log)
    grads = pullback(grad_out.astype(jnp.float32))
    return (grads[0].astype(jnp.bfloat16), grads[1].astype(jnp.bfloat16), grads[2].astype(jnp.bfloat16), grads[3], grads[4], grads[5], grads[6])
```

```python
import functools

import jax
import jax.numpy as jnp
from jax import lax
from jax.experimental import pallas as pl
from jax.experimental.pallas import tpu as pltpu
from jax.sharding import PartitionSpec as P

F32 = jnp.float32
BF16 = jnp.bfloat16
EPS = 1e-06
PAD = 8
RED = 16
GROUP = 2
VMEM_LIMIT = 60 * 1024 * 1024


def split(x):
    hi = x.astype(BF16)
    return hi, (x - hi.astype(F32)).astype(BF16)


def mm(a, b, ta=False, tb=False):
    ah, al = split(a)
    bh, bl = split(b)
    lhs = jnp.concatenate([ah, al], 0 if ta else 1)
    if tb:
        rhs = jnp.concatenate(
            [jnp.concatenate([bh, bh], 1), jnp.concatenate([bl, bl], 1)], 0
        )
    else:
        row = jnp.concatenate([bh, bl], 1)
        rhs = jnp.concatenate([row, row], 0)
    out = lax.dot_general(
        lhs,
        rhs,
        (((0 if ta else 1,), (1 if tb else 0,)), ((), ())),
        preferred_element_type=F32,
    )
    n = out.shape[1] // 2
    return out[:, :n] + out[:, n:]


def ones_mm(ones, x):
    hi, mid = split(x)
    low = (x - hi.astype(F32) - mid.astype(F32)).astype(BF16)
    n = x.shape[1]
    out = jnp.dot(
        ones.astype(BF16), jnp.concatenate([hi, mid, low], 1), preferred_element_type=F32
    )
    return out[:, :n] + out[:, n : 2 * n] + out[:, 2 * n :]


def sigmoid(x):
    return 1.0 / (1.0 + jnp.exp(-x))


def softplus(x):
    return jnp.maximum(x, 0.0) + jnp.log1p(jnp.exp(-jnp.abs(x)))


def iotas(size):
    r = lax.broadcasted_iota(jnp.int32, (size, size), 0)
    c = lax.broadcasted_iota(jnp.int32, (size, size), 1)
    return r, c


def conv_pre(ext, x_ref, halo_ref, w_ref, j, cols):
    size = x_ref.shape[0]
    ext[0:PAD, :] = halo_ref[j, :, cols].astype(F32)
    ext[PAD : PAD + size, :] = x_ref[:, cols].astype(F32)
    taps = w_ref.shape[1]
    rows = [ext[PAD - taps + 1 + i : PAD - taps + 1 + i + size, :] for i in range(taps)]
    pre = w_ref[j, 0:1, cols] * rows[0]
    for i in range(1, taps):
        pre = pre + w_ref[j, i : i + 1, cols] * rows[i]
    return pre, rows


def pick_column(ref, index):
    block = ref[...]
    lane = lax.broadcasted_iota(jnp.int32, block.shape, 1)
    return jnp.sum(jnp.where(lane == index, block, 0.0), axis=1, keepdims=True)


def unit(x):
    r = lax.rsqrt(jnp.sum(x * x, axis=1, keepdims=True) + EPS)
    return x * r, r


def decays(gate, dlog):
    size = gate.shape[0]
    half = size // 2
    r, c = iotas(size)
    speed = -jnp.exp(dlog)
    ld = speed * softplus(gate)
    cum = ones_mm(jnp.where(r >= c, 1.0, 0.0), ld)
    row = lax.broadcasted_iota(jnp.int32, gate.shape, 0)
    first = row < half
    mid = jnp.where(
        first, cum[half // 2 : half // 2 + 1, :], cum[half + half // 2 : half + half // 2 + 1, :]
    )
    edge = cum[half - 1 : half, :]
    last = cum[size - 1 : size, :]
    up = jnp.exp(cum - mid)
    down = jnp.exp(mid - cum)
    cross = jnp.exp(jnp.where(first, edge - cum, cum - edge))
    full = jnp.exp(cum)
    end = jnp.exp(last - cum)
    return ld, speed, up, down, cross, full, end, jnp.exp(last), first


def pair_scores(qk_up, k_down, qk_cross, k_cross):
    size = k_down.shape[0]
    half = size // 2
    same = mm(qk_up, k_down, tb=True)
    other = mm(qk_cross, k_cross, tb=True)
    r, c = iotas(size)
    same_half = (r < half) == (c < half)
    return (
        jnp.where(same_half, same[:size], other[:size]),
        jnp.where(same_half, same[size:], other[size:]),
    )


def unit_inverse(a):
    size = a.shape[0]
    r, c = iotas(size)
    ident = jnp.where(r == c, 1.0, 0.0)
    shift = 3
    small = jnp.where((r >> shift) == (c >> shift), a, 0.0)
    p2 = mm(small, small)
    base = ident - small
    base = base + mm(base, p2)
    p4 = mm(p2, p2)
    d = base + mm(base, p4)
    while (1 << shift) < size:
        joined = ((r >> (shift + 1)) == (c >> (shift + 1))) & ((r >> shift) != (c >> shift))
        d = d - mm(d, mm(jnp.where(joined, a, 0.0), d))
        shift += 1
    return d


def maps_kernel(
    group,
    q_ref, k_ref, v_ref, halo_ref, gate_ref, beta_ref, w_ref, dlog_ref, grad_ref,
    trans_ref, offset_ref, adjoint_ref, inv_ref, raw_ref, att_ref, reach_ref,
    ext,
):
    size = q_ref.shape[0]
    width = trans_ref.shape[1]
    r, c = iotas(size)
    for g in range(group):
        cols = slice(g * width, (g + 1) * width)
        head = pl.program_id(0) * group + g
        pre_q, _ = conv_pre(ext.at[3 * g], q_ref, halo_ref, w_ref, 0, cols)
        pre_k, _ = conv_pre(ext.at[3 * g + 1], k_ref, halo_ref, w_ref, 1, cols)
        pre_v, _ = conv_pre(ext.at[3 * g + 2], v_ref, halo_ref, w_ref, 2, cols)
        q, _ = unit(pre_q * sigmoid(pre_q))
        k, _ = unit(pre_k * sigmoid(pre_k))
        v = pre_v * sigmoid(pre_v)
        beta = sigmoid(pick_column(beta_ref, head))
        ld, speed, up, down, cross, full, end, dend, first = decays(
            gate_ref[:, cols], dlog_ref[:, cols]
        )
        kc = k * cross
        qk_up = jnp.concatenate([q * up, k * up], 0)
        qk_cross = jnp.concatenate([q * cross, kc], 0)
        att, raw = pair_scores(qk_up, k * down, qk_cross, kc)
        att = jnp.where(r >= c, att, 0.0)
        raw = jnp.where(r > c, raw, 0.0)
        inv = unit_inverse(raw * beta)
        by = mm(inv, jnp.concatenate([beta * k * full, beta * v], 1))
        by_k = by[:, :width]
        ends = mm(k * end, by, ta=True)
        rr, cc = iotas(width)
        trans_ref[g] = jnp.where(rr == cc, dend, 0.0) - ends[:, :width]
        offset_ref[g] = ends[:, width:]
        grad = grad_ref[:, cols].astype(F32)
        reach = mm(att, grad, ta=True)
        adjoint_ref[g] = mm(
            jnp.concatenate([q * full, -by_k], 0), jnp.concatenate([grad, reach], 0), ta=True
        )
        inv_ref[g] = inv
        raw_ref[g] = raw
        att_ref[g] = att
        reach_ref[g] = reach


def chain_kernel(
    trans_ref, offset_ref, adjoint_ref, state_ref, cotan_ref,
    send_s, recv_s, send_g, recv_g, ss, rs, sg, rg,
):
    n = lax.axis_size("seq")
    me = lax.axis_index("seq")
    right = lax.rem(me + 1, n)
    left = lax.rem(me + n - 1, n)
    heads = trans_ref.shape[0]
    barrier = pltpu.get_barrier_semaphore()
    for peer in (left, right):
        pl.semaphore_signal(
            barrier, inc=1, device_id={"seq": peer}, device_id_type=pl.DeviceIdType.MESH
        )
    pl.semaphore_wait(barrier, 2)

    def state_copy(h):
        return pltpu.make_async_remote_copy(
            src_ref=send_s.at[h], dst_ref=recv_s.at[h], send_sem=ss.at[h], recv_sem=rs.at[h],
            device_id={"seq": right}, device_id_type=pl.DeviceIdType.MESH,
        )

    def cotan_copy(h):
        return pltpu.make_async_remote_copy(
            src_ref=send_g.at[h], dst_ref=recv_g.at[h], send_sem=sg.at[h], recv_sem=rg.at[h],
            device_id={"seq": left}, device_id_type=pl.DeviceIdType.MESH,
        )

    def forward():
        @pl.loop(0, heads)
        def _(h):
            @pl.when(me == 0)
            def _():
                state_ref[h] = jnp.zeros_like(state_ref[h])
                send_s[h] = offset_ref[h]

            @pl.when(me > 0)
            def _():
                state_copy(h).wait_recv()
                state = recv_s[h]
                state_ref[h] = state
                send_s[h] = mm(trans_ref[h], state) + offset_ref[h]

            @pl.when(me < n - 1)
            def _():
                state_copy(h).start()

    def backward():
        @pl.loop(0, heads)
        def _(h):
            @pl.when(me == n - 1)
            def _():
                cotan_ref[h] = jnp.zeros_like(cotan_ref[h])
                send_g[h] = adjoint_ref[h]

            @pl.when(me < n - 1)
            def _():
                cotan_copy(h).wait_recv()
                cotan = recv_g[h]
                cotan_ref[h] = cotan
                send_g[h] = mm(trans_ref[h], cotan, ta=True) + adjoint_ref[h]

            @pl.when(me > 0)
            def _():
                cotan_copy(h).start()

    @pl.when(me < n // 2)
    def _():
        forward()
        backward()

    @pl.when(me >= n // 2)
    def _():
        backward()
        forward()

    @pl.loop(0, heads)
    def _(h):
        @pl.when(me < n - 1)
        def _():
            state_copy(h).wait_send()

        @pl.when(me > 0)
        def _():
            cotan_copy(h).wait_send()


def grads_kernel(
    group,
    q_ref, k_ref, v_ref, halo_ref, gate_ref, beta_ref, w_ref, dlog_ref, grad_ref,
    inv_ref, raw_ref, att_ref, reach_ref, state_ref, cotan_ref,
    dq_ref, dk_ref, dv_ref, dgate_ref, dbeta_ref, red_ref, tail_ref, last_ref,
    ext, dext,
):
    size = q_ref.shape[0]
    half = size // 2
    width = state_ref.shape[1]
    taps = w_ref.shape[1]
    r, c = iotas(size)
    same_half = (r < half) == (c < half)
    for g in range(group):
        cols = slice(g * width, (g + 1) * width)
        head = pl.program_id(0) * group + g
        pres, rows = [], []
        for j, ref in enumerate((q_ref, k_ref, v_ref)):
            pre, row = conv_pre(ext.at[3 * g + j], ref, halo_ref, w_ref, j, cols)
            pres.append(pre)
            rows.append(row)
        sig = [sigmoid(pre) for pre in pres]
        q, q_r = unit(pres[0] * sig[0])
        k, k_r = unit(pres[1] * sig[1])
        v = pres[2] * sig[2]
        beta = sigmoid(pick_column(beta_ref, head))
        gate = gate_ref[:, cols]
        ld, speed, up, down, cross, full, end, dend, first = decays(gate, dlog_ref[:, cols])
        inv, raw, att, reach = inv_ref[g], raw_ref[g], att_ref[g], reach_ref[g]
        state, cotan = state_ref[g], cotan_ref[g]
        grad = grad_ref[:, cols].astype(F32)

        resid = v - mm(k * full, state)
        deltas = mm(inv, beta * resid)
        d_deltas = reach + mm(k * end, cotan)
        d_err = mm(inv, d_deltas, ta=True)
        d_v = beta * d_err
        stacked = jnp.concatenate([grad, -d_v], 0)
        to_full = mm(stacked, state, tb=True)
        d_qf, d_kf = to_full[:size], to_full[size:]
        scores = mm(jnp.concatenate([grad, -d_err], 0), deltas, tb=True)
        d_att = jnp.where(r >= c, scores[:size], 0.0)
        d_coup = jnp.where(r > c, scores[size:], 0.0)
        d_ke = mm(deltas, cotan, tb=True)
        d_beta = jnp.sum(d_err * resid, axis=1, keepdims=True) + jnp.sum(
            d_coup * raw, axis=1, keepdims=True
        )
        d_raw = d_coup * beta
        kc = k * cross
        both = jnp.concatenate([d_att, d_raw], 0)
        same2 = jnp.concatenate([same_half, same_half], 0)
        d_same = jnp.where(same2, both, 0.0)
        d_other = jnp.where(same2, 0.0, both)
        from_same = mm(d_same, k * down)
        from_other = mm(d_other, kc)
        to_down = mm(d_same, jnp.concatenate([q * up, k * up], 0), ta=True)
        to_cross = mm(d_other, jnp.concatenate([q * cross, kc], 0), ta=True)
        d_q = from_same[:size] * up + from_other[:size] * cross + d_qf * full
        d_k_up = from_same[size:] * up + from_other[size:] * cross + d_kf * full
        k_end_part = d_ke * end
        d_k_down = to_down * down + to_cross * cross + k_end_part
        d_k = d_k_up + d_k_down
        d_cum = q * d_q + k * (d_k_up - d_k_down)
        ones_row = jnp.ones((8, width), F32)
        end_state = mm(ones_row, state * cotan, tb=True)[0:1, :]
        d_last = jnp.sum(k * k_end_part, axis=0, keepdims=True) + dend * end_state
        d_ld = ones_mm(jnp.where(c >= r, 1.0, 0.0), d_cum) + d_last
        dgate_ref[:, cols] = speed * sigmoid(gate) * d_ld
        d_dlog = jnp.sum(ld * d_ld, axis=0, keepdims=True)
        d_braw = d_beta * beta * (1.0 - beta)
        lane = lax.broadcasted_iota(jnp.int32, dbeta_ref.shape, 1)
        dbeta_ref[...] = jnp.where(lane == head, d_braw, dbeta_ref[...])

        d_q = q_r * (d_q - q * jnp.sum(q * d_q, axis=1, keepdims=True))
        d_k = k_r * (d_k - k * jnp.sum(k * d_k, axis=1, keepdims=True))
        red = []
        for j, (d_act, out_ref) in enumerate(((d_q, dq_ref), (d_k, dk_ref), (d_v, dv_ref))):
            s = sig[j]
            d_pre = d_act * (s * (1.0 + pres[j] * (1.0 - s)))
            spot = dext.at[3 * g + j]
            spot[0:PAD, :] = jnp.zeros((PAD, width), F32)
            spot[PAD : PAD + size, :] = d_pre
            spot[PAD + size :, :] = jnp.zeros((PAD, width), F32)
            whole = None
            tail = None
            for i in range(taps):
                w = w_ref[j, i : i + 1, cols]
                start = PAD + taps - 1 - i
                term = w * spot[start : start + size, :]
                edge = w * spot[taps - 1 - i : taps - 1 - i + PAD, :]
                whole = term if whole is None else whole + term
                tail = edge if tail is None else tail + edge
                red.append(jnp.sum(d_pre * rows[j][i], axis=0, keepdims=True))
            out_ref[:, cols] = whole.astype(BF16)
            tail_ref[j, :, cols] = tail
            last_ref[j, :, cols] = whole[size - PAD :, :]
        red.append(d_dlog)
        red.append(jnp.zeros((RED - len(red), width), F32))
        red_ref[g * RED : (g + 1) * RED, :] = jnp.concatenate(red, 0)


def finish_kernel(
    red_ref, tail_ref, total_ref, after_ref,
    parts, mine, result, tail_in, s1, r1, s2, r2, st, rt,
):
    n = lax.axis_size("seq")
    me = lax.axis_index("seq")
    owners = min(n, red_ref.shape[0] // 8)
    piece = red_ref.shape[0] // owners
    right = lax.rem(me + 1, n)
    left = lax.rem(me + n - 1, n)
    mesh_id = pl.DeviceIdType.MESH
    barrier = pltpu.get_barrier_semaphore()

    @pl.loop(1, n)
    def _(step):
        pl.semaphore_signal(
            barrier, inc=1, device_id={"seq": lax.rem(me + step, n)}, device_id_type=mesh_id
        )

    pl.semaphore_wait(barrier, n - 1)

    def rows(owner):
        return pl.ds(pl.multiple_of(owner * piece, 8), piece)

    tail_copy = pltpu.make_async_remote_copy(
        src_ref=tail_ref, dst_ref=tail_in, send_sem=st, recv_sem=rt,
        device_id={"seq": left}, device_id_type=mesh_id,
    )

    def scatter(owner, source):
        return pltpu.make_async_remote_copy(
            src_ref=red_ref.at[rows(owner)], dst_ref=parts.at[source],
            send_sem=s1.at[owner], recv_sem=r1.at[source],
            device_id={"seq": owner}, device_id_type=mesh_id,
        )

    def spread(target, owner):
        return pltpu.make_async_remote_copy(
            src_ref=mine, dst_ref=result.at[rows(owner)],
            send_sem=s2.at[target], recv_sem=r2.at[owner],
            device_id={"seq": target}, device_id_type=mesh_id,
        )

    @pl.loop(0, owners)
    def _(owner):
        @pl.when(owner != me)
        def _():
            scatter(owner, me).start()

    tail_copy.start()

    @pl.when(me < owners)
    def _():
        mine[...] = red_ref[rows(lax.rem(me, owners)), :]

        @pl.loop(0, n)
        def _(source):
            @pl.when(source != me)
            def _():
                scatter(lax.rem(me, owners), source).wait_recv()
                mine[...] += parts[source]

        @pl.loop(1, n)
        def _(step):
            spread(lax.rem(me + step, n), lax.rem(me, owners)).start()

        result[rows(lax.rem(me, owners)), :] = mine[...]

    @pl.loop(0, owners)
    def _(owner):
        @pl.when(owner != me)
        def _():
            spread(me, owner).wait_recv()

    total_ref[...] = result[...]
    tail_copy.wait_recv()
    after_ref[...] = jnp.where(me == n - 1, 0.0, tail_in[...])

    @pl.loop(0, owners)
    def _(owner):
        @pl.when(owner != me)
        def _():
            scatter(owner, me).wait_send()

    @pl.when(me < owners)
    def _():
        @pl.loop(1, n)
        def _(step):
            spread(lax.rem(me + step, n), lax.rem(me, owners)).wait_send()

    tail_copy.wait_send()


def per_device(query_raw, key_raw, value_raw, gate_raw, beta_raw, conv_weight, decay_log, grad_out):
    n = lax.axis_size("seq")
    size, channels = gate_raw.shape
    heads = beta_raw.shape[1]
    width = channels // heads
    group = GROUP if heads % GROUP == 0 else 1
    steps = heads // group
    span = group * width
    dlog = decay_log.reshape(1, channels)
    edges = jnp.stack([x[size - PAD :] for x in (query_raw, key_raw, value_raw)])
    halo = lax.ppermute(edges, "seq", [(i, i + 1) for i in range(n - 1)])

    vmem = pl.BlockSpec(memory_space=pltpu.VMEM)
    tokens = pl.BlockSpec((size, span), lambda h: (0, h))
    rows8 = pl.BlockSpec((3, PAD, span), lambda h: (0, 0, h))
    betas = pl.BlockSpec((size, heads), lambda h: (0, 0))
    weights = pl.BlockSpec((3, conv_weight.shape[1], span), lambda h: (0, 0, h))
    single = pl.BlockSpec((1, span), lambda h: (0, h))
    square = pl.BlockSpec((group, width, width), lambda h: (h, 0, 0))
    pairs = pl.BlockSpec((group, size, size), lambda h: (h, 0, 0))
    tall = pl.BlockSpec((group, size, width), lambda h: (h, 0, 0))
    sq = jax.ShapeDtypeStruct((heads, width, width), F32)
    pr = jax.ShapeDtypeStruct((heads, size, size), F32)
    tl = jax.ShapeDtypeStruct((heads, size, width), F32)
    common = (query_raw, key_raw, value_raw, halo, gate_raw, beta_raw, conv_weight, dlog, grad_out)
    common_specs = [
        tokens, tokens, tokens, rows8, tokens, betas, weights, single, tokens,
    ]
    params = pltpu.CompilerParams(vmem_limit_bytes=VMEM_LIMIT)
    trans, offset, adjoint, inv, raw, att, reach = pl.pallas_call(
        functools.partial(maps_kernel, group),
        grid=(steps,),
        out_shape=(sq, sq, sq, pr, pr, pr, tl),
        in_specs=common_specs,
        out_specs=(square, square, square, pairs, pairs, pairs, tall),
        scratch_shapes=[pltpu.VMEM((3 * group, PAD + size, width), F32)],
        compiler_params=params,
        name="maps",
    )(*common)

    buf = pltpu.VMEM((heads, width, width), F32)
    sems = pltpu.SemaphoreType.DMA((heads,))
    state, cotan = pl.pallas_call(
        chain_kernel,
        out_shape=(sq, sq),
        in_specs=[vmem] * 3,
        out_specs=(vmem, vmem),
        scratch_shapes=[buf] * 4 + [sems] * 4,
        compiler_params=pltpu.CompilerParams(
            collective_id=0, has_side_effects=True, vmem_limit_bytes=VMEM_LIMIT
        ),
        name="chain",
    )(trans, offset, adjoint)

    act = jax.ShapeDtypeStruct((size, channels), BF16)
    edge = jax.ShapeDtypeStruct((3, PAD, channels), F32)
    dq, dk, dv, dgate, dbeta, red, tail, last = pl.pallas_call(
        functools.partial(grads_kernel, group),
        grid=(steps,),
        out_shape=(
            act, act, act,
            jax.ShapeDtypeStruct((size, channels), F32),
            jax.ShapeDtypeStruct((size, heads), F32),
            jax.ShapeDtypeStruct((heads * RED, width), F32),
            edge, edge,
        ),
        in_specs=common_specs + [pairs, pairs, pairs, tall, square, square],
        out_specs=(
            tokens, tokens, tokens, tokens, betas,
            pl.BlockSpec((group * RED, width), lambda h: (h, 0)),
            rows8, rows8,
        ),
        scratch_shapes=[
            pltpu.VMEM((3 * group, PAD + size, width), F32),
            pltpu.VMEM((3 * group, PAD + size + PAD, width), F32),
        ],
        compiler_params=params,
        name="grads",
    )(*common, inv, raw, att, reach, state, cotan)

    owners = min(n, heads * RED // 8)
    piece = heads * RED // owners
    total, after = pl.pallas_call(
        finish_kernel,
        out_shape=(jax.ShapeDtypeStruct(red.shape, F32), edge),
        in_specs=[vmem] * 2,
        out_specs=(vmem, vmem),
        scratch_shapes=[
            pltpu.VMEM((n, piece, width), F32),
            pltpu.VMEM((piece, width), F32),
            pltpu.VMEM(red.shape, F32),
            pltpu.VMEM(edge.shape, F32),
            pltpu.SemaphoreType.DMA((owners,)),
            pltpu.SemaphoreType.DMA((n,)),
            pltpu.SemaphoreType.DMA((n,)),
            pltpu.SemaphoreType.DMA((owners,)),
            pltpu.SemaphoreType.DMA,
            pltpu.SemaphoreType.DMA,
        ],
        compiler_params=pltpu.CompilerParams(
            collective_id=1, has_side_effects=True, vmem_limit_bytes=VMEM_LIMIT
        ),
        name="finish",
    )(red, tail)

    ends = (last + after).astype(BF16)
    dq = lax.dynamic_update_slice(dq, ends[0], (size - PAD, 0))
    dk = lax.dynamic_update_slice(dk, ends[1], (size - PAD, 0))
    dv = lax.dynamic_update_slice(dv, ends[2], (size - PAD, 0))
    taps = conv_weight.shape[1]
    total = total.reshape(heads, RED, width)
    conv_sum = total[:, : 3 * taps].transpose(1, 0, 2).reshape(3, taps, channels)
    decay_sum = total[:, 3 * taps].reshape(channels)
    return (dq, dk, dv, dgate, dbeta, conv_sum, decay_sum)


def solution(mesh):
    in_specs = (
        P("seq", "head"),
        P("seq", "head"),
        P("seq", "head"),
        P("seq", "head"),
        P("seq", "head"),
        P(None, None, "head"),
        P("head"),
        P("seq", "head"),
    )
    out_specs = (
        P("seq", "head"),
        P("seq", "head"),
        P("seq", "head"),
        P("seq", "head"),
        P("seq", "head"),
        P(None, None, "head"),
        P("head"),
    )
    return jax.shard_map(
        per_device, mesh=mesh, in_specs=in_specs, out_specs=out_specs, check_vma=False
    )
```

```python
import functools
import math

import jax
import jax.numpy as jnp
from jax import lax
from jax.experimental import pallas as pl
from jax.experimental.pallas import tpu as pltpu
from jax.sharding import PartitionSpec as P

F32 = jnp.float32
BF16 = jnp.bfloat16
EPS = 1e-06
PAD = 8
RED = 16
GROUP = 4
TEAM = 4
VMEM_LIMIT = 60 * 1024 * 1024


def split(x):
    hi = x.astype(BF16)
    return hi, (x - hi.astype(F32)).astype(BF16)


def mm(a, b, ta=False, tb=False):
    ah, al = split(a)
    bh, bl = split(b)
    lhs = jnp.concatenate([ah, al], 0 if ta else 1)
    if tb:
        rhs = jnp.concatenate(
            [jnp.concatenate([bh, bh], 1), jnp.concatenate([bl, bl], 1)], 0
        )
    else:
        row = jnp.concatenate([bh, bl], 1)
        rhs = jnp.concatenate([row, row], 0)
    out = lax.dot_general(
        lhs,
        rhs,
        (((0 if ta else 1,), (1 if tb else 0,)), ((), ())),
        preferred_element_type=F32,
    )
    n = out.shape[1] // 2
    return out[:, :n] + out[:, n:]


def ones_mm(ones, x):
    hi, mid = split(x)
    low = (x - hi.astype(F32) - mid.astype(F32)).astype(BF16)
    n = x.shape[1]
    out = jnp.dot(
        ones.astype(BF16), jnp.concatenate([hi, mid, low], 1), preferred_element_type=F32
    )
    return out[:, :n] + out[:, n : 2 * n] + out[:, 2 * n :]


def sigmoid(x):
    return 1.0 / (1.0 + jnp.exp(-x))


def softplus(x):
    return jnp.maximum(x, 0.0) + jnp.log1p(jnp.exp(-jnp.abs(x)))


def iotas(size):
    r = lax.broadcasted_iota(jnp.int32, (size, size), 0)
    c = lax.broadcasted_iota(jnp.int32, (size, size), 1)
    return r, c


def conv_pre(ext, x_ref, halo_ref, w_ref, j, cols):
    size = x_ref.shape[0]
    ext[0:PAD, :] = halo_ref[j, :, cols].astype(F32)
    ext[PAD : PAD + size, :] = x_ref[:, cols].astype(F32)
    taps = w_ref.shape[1]
    rows = [ext[PAD - taps + 1 + i : PAD - taps + 1 + i + size, :] for i in range(taps)]
    pre = w_ref[j, 0:1, cols] * rows[0]
    for i in range(1, taps):
        pre = pre + w_ref[j, i : i + 1, cols] * rows[i]
    return pre, rows


def pick_column(ref, index):
    block = ref[...]
    lane = lax.broadcasted_iota(jnp.int32, block.shape, 1)
    return jnp.sum(jnp.where(lane == index, block, 0.0), axis=1, keepdims=True)


def unit(x):
    r = lax.rsqrt(jnp.sum(x * x, axis=1, keepdims=True) + EPS)
    return x * r, r


def decays(gate, dlog):
    size = gate.shape[0]
    half = size // 2
    r, c = iotas(size)
    speed = -jnp.exp(dlog)
    ld = speed * softplus(gate)
    cum = ones_mm(jnp.where(r >= c, 1.0, 0.0), ld)
    row = lax.broadcasted_iota(jnp.int32, gate.shape, 0)
    first = row < half
    mid = jnp.where(
        first, cum[half // 2 : half // 2 + 1, :], cum[half + half // 2 : half + half // 2 + 1, :]
    )
    edge = cum[half - 1 : half, :]
    last = cum[size - 1 : size, :]
    up = jnp.exp(cum - mid)
    down = jnp.exp(mid - cum)
    cross = jnp.exp(jnp.where(first, edge - cum, cum - edge))
    full = jnp.exp(cum)
    end = jnp.exp(last - cum)
    return ld, speed, up, down, cross, full, end, jnp.exp(last), first


def pair_scores(qk_up, k_down, qk_cross, k_cross):
    size = k_down.shape[0]
    half = size // 2
    same = mm(qk_up, k_down, tb=True)
    other = mm(qk_cross, k_cross, tb=True)
    r, c = iotas(size)
    same_half = (r < half) == (c < half)
    return (
        jnp.where(same_half, same[:size], other[:size]),
        jnp.where(same_half, same[size:], other[size:]),
    )


def unit_inverses(coups):
    size = coups[0].shape[0]
    r, c = iotas(size)
    ident = jnp.where(r == c, 1.0, 0.0)
    shift = 3
    inside = (r >> shift) == (c >> shift)
    small = [jnp.where(inside, a, 0.0) for a in coups]
    p2 = [mm(a, a) for a in small]
    base = [ident - a for a in small]
    p4 = [mm(p, p) for p in p2]
    base = [x + mm(x, p) for x, p in zip(base, p2)]
    d = [x + mm(x, p) for x, p in zip(base, p4)]
    while (1 << shift) < size:
        joined = ((r >> (shift + 1)) == (c >> (shift + 1))) & ((r >> shift) != (c >> shift))
        low = [mm(jnp.where(joined, a, 0.0), x) for a, x in zip(coups, d)]
        d = [x - mm(x, y) for x, y in zip(d, low)]
        shift += 1
    return d


def maps_kernel(
    group,
    q_ref, k_ref, v_ref, halo_ref, gate_ref, beta_ref, w_ref, dlog_ref, grad_ref,
    trans_ref, offset_ref, adjoint_ref, inv_ref, raw_ref, att_ref, reach_ref,
    ext,
):
    size = q_ref.shape[0]
    width = trans_ref.shape[1]
    r, c = iotas(size)
    held = []
    for g in range(group):
        cols = slice(g * width, (g + 1) * width)
        head = pl.program_id(0) * group + g
        pre_q, _ = conv_pre(ext.at[3 * g], q_ref, halo_ref, w_ref, 0, cols)
        pre_k, _ = conv_pre(ext.at[3 * g + 1], k_ref, halo_ref, w_ref, 1, cols)
        pre_v, _ = conv_pre(ext.at[3 * g + 2], v_ref, halo_ref, w_ref, 2, cols)
        q, _ = unit(pre_q * sigmoid(pre_q))
        k, _ = unit(pre_k * sigmoid(pre_k))
        v = pre_v * sigmoid(pre_v)
        beta = sigmoid(pick_column(beta_ref, head))
        ld, speed, up, down, cross, full, end, dend, first = decays(
            gate_ref[:, cols], dlog_ref[:, cols]
        )
        kc = k * cross
        qk_up = jnp.concatenate([q * up, k * up], 0)
        qk_cross = jnp.concatenate([q * cross, kc], 0)
        att, raw = pair_scores(qk_up, k * down, qk_cross, kc)
        att = jnp.where(r >= c, att, 0.0)
        raw = jnp.where(r > c, raw, 0.0)
        raw_ref[g] = raw
        att_ref[g] = att
        reach_ref[g] = mm(att, grad_ref[:, cols].astype(F32), ta=True)
        inputs = jnp.concatenate([beta * k * full, beta * v], 1)
        held.append((raw * beta, inputs, k * end, dend, q * full))
    invs = unit_inverses([item[0] for item in held])
    bys = [mm(inv, item[1]) for inv, item in zip(invs, held)]
    rr, cc = iotas(width)
    for g in range(group):
        cols = slice(g * width, (g + 1) * width)
        inv_ref[g] = invs[g]
        ends = mm(held[g][2], bys[g], ta=True)
        trans_ref[g] = jnp.where(rr == cc, held[g][3], 0.0) - ends[:, :width]
        offset_ref[g] = ends[:, width:]
        adjoint_ref[g] = mm(
            jnp.concatenate([held[g][4], -bys[g][:, :width]], 0),
            jnp.concatenate([grad_ref[:, cols].astype(F32), reach_ref[g]], 0),
            ta=True,
        )


def chain_kernel(
    trans_ref, offset_ref, adjoint_ref, state_ref, cotan_ref,
    gt, gb, ga, pre_t, pre_b, send_s, send_g, in_s, in_g, out_s, out_g, back_s, back_g,
    at_s, at_r, ab_s, ab_r, aa_s, aa_r, ss, rs, sg, rg, bs_s, bs_r, bg_s, bg_r,
):
    n = lax.axis_size("seq")
    me = lax.axis_index("seq")
    team, mine_heads = gt.shape[0], gt.shape[1]
    mine = lax.rem(me, team)
    base = me - mine
    level = me // team
    levels = n // team
    mesh_id = pl.DeviceIdType.MESH
    after = lax.rem(me + team, n)
    ahead = lax.rem(me + n - team, n)
    barrier = pltpu.get_barrier_semaphore()
    peers = [base + lax.rem(mine + i, team) for i in range(1, team)]
    links = peers + ([after, ahead] if levels > 1 else [])
    for peer in links:
        pl.semaphore_signal(barrier, inc=1, device_id={"seq": peer}, device_id_type=mesh_id)
    pl.semaphore_wait(barrier, len(links))

    def block(member):
        return pl.ds(member * mine_heads, mine_heads)

    def spread(source, target, ref, dst, send, recv):
        return pltpu.make_async_remote_copy(
            src_ref=ref.at[block(target)], dst_ref=dst.at[source],
            send_sem=send.at[target], recv_sem=recv.at[source],
            device_id={"seq": base + target}, device_id_type=mesh_id,
        )

    kinds = (
        (trans_ref, gt, at_s, at_r), (offset_ref, gb, ab_s, ab_r), (adjoint_ref, ga, aa_s, aa_r)
    )
    others = [lax.rem(mine + i, team) for i in range(1, team)]
    for kind in kinds:
        for other in others:
            spread(mine, other, *kind).start()
    for ref, dst, _, _ in kinds:
        dst[mine] = ref[block(mine)]
    for kind in kinds[:2]:
        for other in others:
            spread(other, other, *kind).wait_recv()

    for h in range(mine_heads):
        pre_t[0, h] = gt[0, h]
        pre_b[0, h] = gb[0, h]
    for j in range(1, team):
        for h in range(mine_heads):
            both = mm(gt[j, h], jnp.concatenate([pre_t[j - 1, h], pre_b[j - 1, h]], 1))
            width = both.shape[1] // 2
            pre_t[j, h] = both[:, :width]
            pre_b[j, h] = both[:, width:] + gb[j, h]
    for other in others:
        spread(other, other, *kinds[2]).wait_recv()
    for h in range(mine_heads):
        send_g[h] = ga[team - 1, h]
    for j in range(team - 2, -1, -1):
        for h in range(mine_heads):
            send_g[h] = mm(gt[j, h], send_g[h], ta=True) + ga[j, h]

    def state_copy(h):
        return pltpu.make_async_remote_copy(
            src_ref=send_s.at[h], dst_ref=in_s.at[h], send_sem=ss.at[h], recv_sem=rs.at[h],
            device_id={"seq": after}, device_id_type=mesh_id,
        )

    def cotan_copy(h):
        return pltpu.make_async_remote_copy(
            src_ref=send_g.at[h], dst_ref=in_g.at[h], send_sem=sg.at[h], recv_sem=rg.at[h],
            device_id={"seq": ahead}, device_id_type=mesh_id,
        )

    def give(member, owner, src, dst, send, recv):
        return pltpu.make_async_remote_copy(
            src_ref=src.at[member], dst_ref=dst.at[block(owner)],
            send_sem=send.at[member], recv_sem=recv.at[owner],
            device_id={"seq": base + member}, device_id_type=mesh_id,
        )

    states = (out_s, back_s, bs_s, bs_r)
    cotans = (out_g, back_g, bg_s, bg_r)

    def forward():
        for h in range(mine_heads):
            @pl.when(level == 0)
            def _():
                out_s[0, h] = jnp.zeros_like(out_s[0, h])
                send_s[h] = pre_b[team - 1, h]

            @pl.when(level > 0)
            def _():
                state_copy(h).wait_recv()
                state = in_s[h]
                out_s[0, h] = state

                @pl.when(level < levels - 1)
                def _():
                    send_s[h] = mm(pre_t[team - 1, h], state) + pre_b[team - 1, h]

            @pl.when(level < levels - 1)
            def _():
                state_copy(h).start()

        for j in range(1, team):
            for h in range(mine_heads):
                out_s[j, h] = mm(pre_t[j - 1, h], out_s[0, h]) + pre_b[j - 1, h]
        for other in others:
            give(other, mine, *states).start()

    def backward():
        for h in range(mine_heads):
            @pl.when(level == levels - 1)
            def _():
                out_g[team - 1, h] = jnp.zeros_like(out_g[0, h])

            @pl.when(level < levels - 1)
            def _():
                cotan_copy(h).wait_recv()
                cotan = in_g[h]
                out_g[team - 1, h] = cotan

                @pl.when(level > 0)
                def _():
                    send_g[h] = mm(pre_t[team - 1, h], cotan, ta=True) + send_g[h]

            @pl.when(level > 0)
            def _():
                cotan_copy(h).start()

        for j in range(team - 1, 0, -1):
            for h in range(mine_heads):
                out_g[j - 1, h] = mm(gt[j, h], out_g[j, h], ta=True) + ga[j, h]

        for other in others:
            give(other, mine, *cotans).start()

    @pl.when(level < levels // 2)
    def _():
        forward()
        backward()

    @pl.when(level >= levels // 2)
    def _():
        backward()
        forward()

    back_s[block(mine)] = out_s[mine]
    back_g[block(mine)] = out_g[mine]
    for other in others:
        give(mine, other, *states).wait_recv()
    for other in others:
        give(mine, other, *cotans).wait_recv()
    state_ref[...] = back_s[...]
    cotan_ref[...] = back_g[...]
    for other in others:
        for kind in kinds:
            spread(mine, other, *kind).wait_send()
        give(other, mine, *states).wait_send()
        give(other, mine, *cotans).wait_send()
    for h in range(mine_heads):
        @pl.when(level < levels - 1)
        def _():
            state_copy(h).wait_send()

        @pl.when(level > 0)
        def _():
            cotan_copy(h).wait_send()


def grads_kernel(
    group,
    q_ref, k_ref, v_ref, halo_ref, gate_ref, beta_ref, w_ref, dlog_ref, grad_ref,
    inv_ref, raw_ref, att_ref, reach_ref, state_ref, cotan_ref,
    dq_ref, dk_ref, dv_ref, dgate_ref, dbeta_ref, red_ref, tail_ref, last_ref,
    ext, dext,
):
    size = q_ref.shape[0]
    half = size // 2
    width = state_ref.shape[1]
    taps = w_ref.shape[1]
    r, c = iotas(size)
    same_half = (r < half) == (c < half)
    for g in range(group):
        cols = slice(g * width, (g + 1) * width)
        head = pl.program_id(0) * group + g
        pres, rows = [], []
        for j, ref in enumerate((q_ref, k_ref, v_ref)):
            pre, row = conv_pre(ext.at[3 * g + j], ref, halo_ref, w_ref, j, cols)
            pres.append(pre)
            rows.append(row)
        sig = [sigmoid(pre) for pre in pres]
        q, q_r = unit(pres[0] * sig[0])
        k, k_r = unit(pres[1] * sig[1])
        v = pres[2] * sig[2]
        beta = sigmoid(pick_column(beta_ref, head))
        gate = gate_ref[:, cols]
        ld, speed, up, down, cross, full, end, dend, first = decays(gate, dlog_ref[:, cols])
        inv, raw, att, reach = inv_ref[g], raw_ref[g], att_ref[g], reach_ref[g]
        state, cotan = state_ref[g], cotan_ref[g]
        grad = grad_ref[:, cols].astype(F32)

        resid = v - mm(k * full, state)
        deltas = mm(inv, beta * resid)
        d_deltas = reach + mm(k * end, cotan)
        d_err = mm(inv, d_deltas, ta=True)
        d_v = beta * d_err
        stacked = jnp.concatenate([grad, -d_v], 0)
        to_full = mm(stacked, state, tb=True)
        d_qf, d_kf = to_full[:size], to_full[size:]
        scores = mm(jnp.concatenate([grad, -d_err], 0), deltas, tb=True)
        d_att = jnp.where(r >= c, scores[:size], 0.0)
        d_coup = jnp.where(r > c, scores[size:], 0.0)
        d_ke = mm(deltas, cotan, tb=True)
        d_beta = jnp.sum(d_err * resid, axis=1, keepdims=True) + jnp.sum(
            d_coup * raw, axis=1, keepdims=True
        )
        d_raw = d_coup * beta
        kc = k * cross
        both = jnp.concatenate([d_att, d_raw], 0)
        same2 = jnp.concatenate([same_half, same_half], 0)
        d_same = jnp.where(same2, both, 0.0)
        d_other = jnp.where(same2, 0.0, both)
        from_same = mm(d_same, k * down)
        from_other = mm(d_other, kc)
        to_down = mm(d_same, jnp.concatenate([q * up, k * up], 0), ta=True)
        to_cross = mm(d_other, jnp.concatenate([q * cross, kc], 0), ta=True)
        d_q = from_same[:size] * up + from_other[:size] * cross + d_qf * full
        d_k_up = from_same[size:] * up + from_other[size:] * cross + d_kf * full
        k_end_part = d_ke * end
        d_k_down = to_down * down + to_cross * cross + k_end_part
        d_k = d_k_up + d_k_down
        d_cum = q * d_q + k * (d_k_up - d_k_down)
        ones_row = jnp.ones((8, width), F32)
        end_state = mm(ones_row, state * cotan, tb=True)[0:1, :]
        d_last = jnp.sum(k * k_end_part, axis=0, keepdims=True) + dend * end_state
        d_ld = ones_mm(jnp.where(c >= r, 1.0, 0.0), d_cum) + d_last
        dgate_ref[:, cols] = speed * sigmoid(gate) * d_ld
        d_dlog = jnp.sum(ld * d_ld, axis=0, keepdims=True)
        d_braw = d_beta * beta * (1.0 - beta)
        lane = lax.broadcasted_iota(jnp.int32, dbeta_ref.shape, 1)
        dbeta_ref[...] = jnp.where(lane == head, d_braw, dbeta_ref[...])

        d_q = q_r * (d_q - q * jnp.sum(q * d_q, axis=1, keepdims=True))
        d_k = k_r * (d_k - k * jnp.sum(k * d_k, axis=1, keepdims=True))
        red = []
        for j, (d_act, out_ref) in enumerate(((d_q, dq_ref), (d_k, dk_ref), (d_v, dv_ref))):
            s = sig[j]
            d_pre = d_act * (s * (1.0 + pres[j] * (1.0 - s)))
            spot = dext.at[3 * g + j]
            spot[0:PAD, :] = jnp.zeros((PAD, width), F32)
            spot[PAD : PAD + size, :] = d_pre
            spot[PAD + size :, :] = jnp.zeros((PAD, width), F32)
            whole = None
            tail = None
            for i in range(taps):
                w = w_ref[j, i : i + 1, cols]
                start = PAD + taps - 1 - i
                term = w * spot[start : start + size, :]
                edge = w * spot[taps - 1 - i : taps - 1 - i + PAD, :]
                whole = term if whole is None else whole + term
                tail = edge if tail is None else tail + edge
                red.append(jnp.sum(d_pre * rows[j][i], axis=0, keepdims=True))
            out_ref[:, cols] = whole.astype(BF16)
            tail_ref[j, :, cols] = tail
            last_ref[j, :, cols] = whole[size - PAD :, :]
        red.append(d_dlog)
        red.append(jnp.zeros((RED - len(red), width), F32))
        red_ref[g * RED : (g + 1) * RED, :] = jnp.concatenate(red, 0)


def finish_kernel(
    red_ref, tail_ref, conv_ref, decay_ref, after_ref,
    parts, mine, result, tail_in, s1, r1, s2, r2, st, rt,
):
    n = lax.axis_size("seq")
    me = lax.axis_index("seq")
    owners = min(n, red_ref.shape[0] // 8)
    piece = red_ref.shape[0] // owners
    right = lax.rem(me + 1, n)
    left = lax.rem(me + n - 1, n)
    mesh_id = pl.DeviceIdType.MESH
    barrier = pltpu.get_barrier_semaphore()

    @pl.loop(1, n)
    def _(step):
        pl.semaphore_signal(
            barrier, inc=1, device_id={"seq": lax.rem(me + step, n)}, device_id_type=mesh_id
        )

    pl.semaphore_wait(barrier, n - 1)

    def rows(owner):
        return pl.ds(pl.multiple_of(owner * piece, 8), piece)

    tail_copy = pltpu.make_async_remote_copy(
        src_ref=tail_ref, dst_ref=tail_in, send_sem=st, recv_sem=rt,
        device_id={"seq": left}, device_id_type=mesh_id,
    )

    def scatter(owner, source):
        return pltpu.make_async_remote_copy(
            src_ref=red_ref.at[rows(owner)], dst_ref=parts.at[source],
            send_sem=s1.at[owner], recv_sem=r1.at[source],
            device_id={"seq": owner}, device_id_type=mesh_id,
        )

    def spread(target, owner):
        return pltpu.make_async_remote_copy(
            src_ref=mine, dst_ref=result.at[rows(owner)],
            send_sem=s2.at[target], recv_sem=r2.at[owner],
            device_id={"seq": target}, device_id_type=mesh_id,
        )

    @pl.loop(0, owners)
    def _(owner):
        @pl.when(owner != me)
        def _():
            scatter(owner, me).start()

    tail_copy.start()

    @pl.when(me < owners)
    def _():
        mine[...] = red_ref[rows(lax.rem(me, owners)), :]

        @pl.loop(0, n)
        def _(source):
            @pl.when(source != me)
            def _():
                scatter(lax.rem(me, owners), source).wait_recv()
                mine[...] += parts[source]

        @pl.loop(1, n)
        def _(step):
            spread(lax.rem(me + step, n), lax.rem(me, owners)).start()

        result[rows(lax.rem(me, owners)), :] = mine[...]

    @pl.loop(0, owners)
    def _(owner):
        @pl.when(owner != me)
        def _():
            spread(me, owner).wait_recv()

    width = result.shape[1]
    taps = conv_ref.shape[1]
    for h in range(result.shape[0] // RED):
        cols = slice(h * width, (h + 1) * width)
        for j in range(3):
            start = h * RED + j * taps
            conv_ref[j, :, cols] = result[start : start + taps, :]
        start = h * RED + 3 * taps
        decay_ref[:, cols] = result[start : start + 1, :]
    tail_copy.wait_recv()
    after_ref[...] = jnp.where(me == n - 1, 0.0, tail_in[...])

    @pl.loop(0, owners)
    def _(owner):
        @pl.when(owner != me)
        def _():
            scatter(owner, me).wait_send()

    @pl.when(me < owners)
    def _():
        @pl.loop(1, n)
        def _(step):
            spread(lax.rem(me + step, n), lax.rem(me, owners)).wait_send()

    tail_copy.wait_send()


def per_device(query_raw, key_raw, value_raw, gate_raw, beta_raw, conv_weight, decay_log, grad_out):
    n = lax.axis_size("seq")
    size, channels = gate_raw.shape
    heads = beta_raw.shape[1]
    width = channels // heads
    group = GROUP if heads % GROUP == 0 else 1
    steps = heads // group
    span = group * width
    dlog = decay_log.reshape(1, channels)
    edges = jnp.stack([x[size - PAD :] for x in (query_raw, key_raw, value_raw)])
    halo = lax.ppermute(edges, "seq", [(i, i + 1) for i in range(n - 1)])

    vmem = pl.BlockSpec(memory_space=pltpu.VMEM)
    tokens = pl.BlockSpec((size, span), lambda h: (0, h))
    rows8 = pl.BlockSpec((3, PAD, span), lambda h: (0, 0, h))
    betas = pl.BlockSpec((size, heads), lambda h: (0, 0))
    weights = pl.BlockSpec((3, conv_weight.shape[1], span), lambda h: (0, 0, h))
    single = pl.BlockSpec((1, span), lambda h: (0, h))
    square = pl.BlockSpec((group, width, width), lambda h: (h, 0, 0))
    pairs = pl.BlockSpec((group, size, size), lambda h: (h, 0, 0))
    tall = pl.BlockSpec((group, size, width), lambda h: (h, 0, 0))
    sq = jax.ShapeDtypeStruct((heads, width, width), F32)
    pr = jax.ShapeDtypeStruct((heads, size, size), F32)
    tl = jax.ShapeDtypeStruct((heads, size, width), F32)
    common = (query_raw, key_raw, value_raw, halo, gate_raw, beta_raw, conv_weight, dlog, grad_out)
    common_specs = [
        tokens, tokens, tokens, rows8, tokens, betas, weights, single, tokens,
    ]
    params = pltpu.CompilerParams(vmem_limit_bytes=VMEM_LIMIT)
    trans, offset, adjoint, inv, raw, att, reach = pl.pallas_call(
        functools.partial(maps_kernel, group),
        grid=(steps,),
        out_shape=(sq, sq, sq, pr, pr, pr, tl),
        in_specs=common_specs,
        out_specs=(square, square, square, pairs, pairs, pairs, tall),
        scratch_shapes=[pltpu.VMEM((3 * group, PAD + size, width), F32)],
        compiler_params=params,
        name="maps",
    )(*common)

    team = math.gcd(TEAM, math.gcd(n, heads))
    part = heads // team
    whole = pltpu.VMEM((heads, width, width), F32)
    few = pltpu.VMEM((part, width, width), F32)
    many = pltpu.VMEM((team, part, width, width), F32)
    sems = pltpu.SemaphoreType.DMA((team,))
    hops = pltpu.SemaphoreType.DMA((part,))
    state, cotan = pl.pallas_call(
        chain_kernel,
        out_shape=(sq, sq),
        in_specs=[vmem] * 3,
        out_specs=(vmem, vmem),
        scratch_shapes=[many] * 5 + [few] * 4 + [many] * 2 + [whole] * 2
        + [sems] * 6 + [hops] * 4 + [sems] * 4,
        compiler_params=pltpu.CompilerParams(
            collective_id=0, has_side_effects=True, vmem_limit_bytes=VMEM_LIMIT
        ),
        name="chain",
    )(trans, offset, adjoint)

    act = jax.ShapeDtypeStruct((size, channels), BF16)
    edge = jax.ShapeDtypeStruct((3, PAD, channels), F32)
    dq, dk, dv, dgate, dbeta, red, tail, last = pl.pallas_call(
        functools.partial(grads_kernel, group),
        grid=(steps,),
        out_shape=(
            act, act, act,
            jax.ShapeDtypeStruct((size, channels), F32),
            jax.ShapeDtypeStruct((size, heads), F32),
            jax.ShapeDtypeStruct((heads * RED, width), F32),
            edge, edge,
        ),
        in_specs=common_specs + [pairs, pairs, pairs, tall, square, square],
        out_specs=(
            tokens, tokens, tokens, tokens, betas,
            pl.BlockSpec((group * RED, width), lambda h: (h, 0)),
            rows8, rows8,
        ),
        scratch_shapes=[
            pltpu.VMEM((3 * group, PAD + size, width), F32),
            pltpu.VMEM((3 * group, PAD + size + PAD, width), F32),
        ],
        compiler_params=params,
        name="grads",
    )(*common, inv, raw, att, reach, state, cotan)

    owners = min(n, heads * RED // 8)
    piece = heads * RED // owners
    conv_sum, decay_sum, after = pl.pallas_call(
        finish_kernel,
        out_shape=(
            jax.ShapeDtypeStruct(conv_weight.shape, F32),
            jax.ShapeDtypeStruct((1, channels), F32),
            edge,
        ),
        in_specs=[vmem] * 2,
        out_specs=(vmem, vmem, vmem),
        scratch_shapes=[
            pltpu.VMEM((n, piece, width), F32),
            pltpu.VMEM((piece, width), F32),
            pltpu.VMEM(red.shape, F32),
            pltpu.VMEM(edge.shape, F32),
            pltpu.SemaphoreType.DMA((owners,)),
            pltpu.SemaphoreType.DMA((n,)),
            pltpu.SemaphoreType.DMA((n,)),
            pltpu.SemaphoreType.DMA((owners,)),
            pltpu.SemaphoreType.DMA,
            pltpu.SemaphoreType.DMA,
        ],
        compiler_params=pltpu.CompilerParams(
            collective_id=1, has_side_effects=True, vmem_limit_bytes=VMEM_LIMIT
        ),
        name="finish",
    )(red, tail)

    ends = (last + after).astype(BF16)
    dq = lax.dynamic_update_slice(dq, ends[0], (size - PAD, 0))
    dk = lax.dynamic_update_slice(dk, ends[1], (size - PAD, 0))
    dv = lax.dynamic_update_slice(dv, ends[2], (size - PAD, 0))
    return (dq, dk, dv, dgate, dbeta, conv_sum, decay_sum.reshape(channels))


def solution(mesh):
    in_specs = (
        P("seq", "head"),
        P("seq", "head"),
        P("seq", "head"),
        P("seq", "head"),
        P("seq", "head"),
        P(None, None, "head"),
        P("head"),
        P("seq", "head"),
    )
    out_specs = (
        P("seq", "head"),
        P("seq", "head"),
        P("seq", "head"),
        P("seq", "head"),
        P("seq", "head"),
        P(None, None, "head"),
        P("head"),
    )
    return jax.shard_map(
        per_device, mesh=mesh, in_specs=in_specs, out_specs=out_specs, check_vma=False
    )
```

```python
import functools
import math

import jax
import jax.numpy as jnp
from jax import lax
from jax.experimental import pallas as pl
from jax.experimental.pallas import tpu as pltpu
from jax.sharding import PartitionSpec as P

F32 = jnp.float32
BF16 = jnp.bfloat16
EPS = 1e-06
PAD = 8
RED = 16
GROUP = 4
GROUP_MAPS = 4
LINK = F32
TEAM = 4
VMEM_LIMIT = 60 * 1024 * 1024


def split(x):
    hi = x.astype(BF16)
    return hi, (x - hi.astype(F32)).astype(BF16)


def mm(a, b, ta=False, tb=False):
    ah, al = split(a)
    bh, bl = split(b)
    lhs = jnp.concatenate([ah, al], 0 if ta else 1)
    if tb:
        rhs = jnp.concatenate(
            [jnp.concatenate([bh, bh], 1), jnp.concatenate([bl, bl], 1)], 0
        )
    else:
        row = jnp.concatenate([bh, bl], 1)
        rhs = jnp.concatenate([row, row], 0)
    out = lax.dot_general(
        lhs,
        rhs,
        (((0 if ta else 1,), (1 if tb else 0,)), ((), ())),
        preferred_element_type=F32,
    )
    n = out.shape[1] // 2
    return out[:, :n] + out[:, n:]


def ones_mm(ones, x):
    hi, mid = split(x)
    low = (x - hi.astype(F32) - mid.astype(F32)).astype(BF16)
    n = x.shape[1]
    out = jnp.dot(
        ones.astype(BF16), jnp.concatenate([hi, mid, low], 1), preferred_element_type=F32
    )
    return out[:, :n] + out[:, n : 2 * n] + out[:, 2 * n :]


def sigmoid(x):
    return 1.0 / (1.0 + jnp.exp(-x))


def softplus(x):
    return jnp.maximum(x, 0.0) + jnp.log1p(jnp.exp(-jnp.abs(x)))


def iotas(size):
    r = lax.broadcasted_iota(jnp.int32, (size, size), 0)
    c = lax.broadcasted_iota(jnp.int32, (size, size), 1)
    return r, c


def conv_pre(ext, x_ref, halo_ref, w_ref, j, cols):
    size = x_ref.shape[0]
    ext[0:PAD, :] = halo_ref[j, :, cols].astype(F32)
    ext[PAD : PAD + size, :] = x_ref[:, cols].astype(F32)
    taps = w_ref.shape[1]
    rows = [ext[PAD - taps + 1 + i : PAD - taps + 1 + i + size, :] for i in range(taps)]
    pre = w_ref[j, 0:1, cols] * rows[0]
    for i in range(1, taps):
        pre = pre + w_ref[j, i : i + 1, cols] * rows[i]
    return pre, rows


def pick_column(ref, index):
    block = ref[...]
    lane = lax.broadcasted_iota(jnp.int32, block.shape, 1)
    return jnp.sum(jnp.where(lane == index, block, 0.0), axis=1, keepdims=True)


def unit(x):
    r = lax.rsqrt(jnp.sum(x * x, axis=1, keepdims=True) + EPS)
    return x * r, r


def decays(gate, dlog):
    size = gate.shape[0]
    half = size // 2
    r, c = iotas(size)
    speed = -jnp.exp(dlog)
    ld = speed * softplus(gate)
    cum = ones_mm(jnp.where(r >= c, 1.0, 0.0), ld)
    row = lax.broadcasted_iota(jnp.int32, gate.shape, 0)
    first = row < half
    mid = jnp.where(
        first, cum[half // 2 : half // 2 + 1, :], cum[half + half // 2 : half + half // 2 + 1, :]
    )
    edge = cum[half - 1 : half, :]
    last = cum[size - 1 : size, :]
    up = jnp.exp(cum - mid)
    down = jnp.exp(mid - cum)
    cross = jnp.exp(jnp.where(first, edge - cum, cum - edge))
    full = jnp.exp(cum)
    end = jnp.exp(last - cum)
    return ld, speed, up, down, cross, full, end, jnp.exp(last), first


def pair_scores(qk_up, k_down, qk_cross, k_cross):
    size = k_down.shape[0]
    half = size // 2
    same = mm(qk_up, k_down, tb=True)
    other = mm(qk_cross, k_cross, tb=True)
    r, c = iotas(size)
    same_half = (r < half) == (c < half)
    return (
        jnp.where(same_half, same[:size], other[:size]),
        jnp.where(same_half, same[size:], other[size:]),
    )


def unit_inverses(coups):
    size = coups[0].shape[0]
    r, c = iotas(size)
    ident = jnp.where(r == c, 1.0, 0.0)
    shift = 3
    inside = (r >> shift) == (c >> shift)
    small = [jnp.where(inside, a, 0.0) for a in coups]
    p2 = [mm(a, a) for a in small]
    base = [ident - a for a in small]
    p4 = [mm(p, p) for p in p2]
    base = [x + mm(x, p) for x, p in zip(base, p2)]
    d = [x + mm(x, p) for x, p in zip(base, p4)]
    while (1 << shift) < size:
        joined = ((r >> (shift + 1)) == (c >> (shift + 1))) & ((r >> shift) != (c >> shift))
        low = [mm(jnp.where(joined, a, 0.0), x) for a, x in zip(coups, d)]
        d = [x - mm(x, y) for x, y in zip(d, low)]
        shift += 1
    return d


def scan_kernel(
    group,
    q_ref, k_ref, v_ref, gate_ref, beta_ref, w_ref, dlog_ref, grad_ref,
    halo_ref, inv_ref, raw_ref, att_ref, reach_ref, state_ref, cotan_ref,
    ext, halo_in, trans, offset, adjoint,
    gt, gb, ga, pre_t, pre_b, send_s, send_g, in_s, in_g, out_s, out_g, back_s, back_g,
    hs, hr, at_s, at_r, ab_s, ab_r, aa_s, aa_r, ss, rs, sg, rg, bs_s, bs_r, bg_s, bg_r,
):
    n = lax.axis_size("seq")
    me = lax.axis_index("seq")
    team, mine_heads = gt.shape[0], gt.shape[1]
    mine = lax.rem(me, team)
    base = me - mine
    level = me // team
    levels = n // team
    mesh_id = pl.DeviceIdType.MESH
    right = lax.rem(me + 1, n)
    left = lax.rem(me + n - 1, n)
    after = lax.rem(me + team, n)
    ahead = lax.rem(me + n - team, n)
    barrier = pltpu.get_barrier_semaphore()
    peers = [base + lax.rem(mine + i, team) for i in range(1, team)]
    links = peers + [right, left] + ([after, ahead] if levels > 1 else [])
    for peer in links:
        pl.semaphore_signal(barrier, inc=1, device_id={"seq": peer}, device_id_type=mesh_id)
    pl.semaphore_wait(barrier, len(links))

    size = q_ref.shape[0]
    heads, width = trans.shape[0], trans.shape[1]

    def halo_copy(j, ref):
        return pltpu.make_async_remote_copy(
            src_ref=ref.at[pl.ds(size - PAD, PAD)], dst_ref=halo_in.at[j],
            send_sem=hs.at[j], recv_sem=hr.at[j],
            device_id={"seq": right}, device_id_type=mesh_id,
        )

    @pl.when(me < n - 1)
    def _():
        for j, ref in enumerate((q_ref, k_ref, v_ref)):
            halo_copy(j, ref).start()

    def block(member):
        return pl.ds(member * mine_heads, mine_heads)

    def spread(source, target, ref, dst, send, recv):
        return pltpu.make_async_remote_copy(
            src_ref=ref.at[block(target)], dst_ref=dst.at[source],
            send_sem=send.at[target], recv_sem=recv.at[source],
            device_id={"seq": base + target}, device_id_type=mesh_id,
        )

    kinds = (
        (trans, gt, at_s, at_r), (offset, gb, ab_s, ab_r), (adjoint, ga, aa_s, aa_r)
    )
    others = [lax.rem(mine + i, team) for i in range(1, team)]
    order = others + [mine]
    r, c = iotas(size)
    rr, cc = iotas(width)
    for begin in range(0, heads, group):
        held = []
        places = []
        for g in range(group):
            at = begin + g
            head = order[at // mine_heads] * mine_heads + at % mine_heads
            places.append((head, pl.ds(pl.multiple_of(head * width, width), width)))
        fades = [decays(gate_ref[:, cols], dlog_ref[:, cols]) for _, cols in places]
        if begin == 0:
            @pl.when(me == 0)
            def _():
                halo_in[...] = jnp.zeros_like(halo_in)

            @pl.when(me > 0)
            def _():
                for j, ref in enumerate((q_ref, k_ref, v_ref)):
                    halo_copy(j, ref).wait_recv()

            halo_ref[...] = halo_in[...]
        for g, (head, cols) in enumerate(places):
            pre_q, _ = conv_pre(ext.at[3 * g], q_ref, halo_in, w_ref, 0, cols)
            pre_k, _ = conv_pre(ext.at[3 * g + 1], k_ref, halo_in, w_ref, 1, cols)
            pre_v, _ = conv_pre(ext.at[3 * g + 2], v_ref, halo_in, w_ref, 2, cols)
            q, _ = unit(pre_q * sigmoid(pre_q))
            k, _ = unit(pre_k * sigmoid(pre_k))
            v = pre_v * sigmoid(pre_v)
            beta = sigmoid(pick_column(beta_ref, head))
            ld, speed, up, down, cross, full, end, dend, first = fades[g]
            kc = k * cross
            qk_up = jnp.concatenate([q * up, k * up], 0)
            qk_cross = jnp.concatenate([q * cross, kc], 0)
            att, raw = pair_scores(qk_up, k * down, qk_cross, kc)
            att = jnp.where(r >= c, att, 0.0)
            raw = jnp.where(r > c, raw, 0.0)
            raw_ref[head] = raw
            att_ref[head] = att
            reach_ref[head] = mm(att, grad_ref[:, cols].astype(F32), ta=True)
            inputs = jnp.concatenate([beta * k * full, beta * v], 1)
            held.append((raw * beta, inputs, k * end, dend, q * full))
        invs = unit_inverses([item[0] for item in held])
        bys = [mm(inv, item[1]) for inv, item in zip(invs, held)]
        for g, (head, cols) in enumerate(places):
            inv_ref[head] = invs[g]
            ends = mm(held[g][2], bys[g], ta=True)
            trans[head] = (jnp.where(rr == cc, held[g][3], 0.0) - ends[:, :width]).astype(LINK)
            offset[head] = ends[:, width:].astype(LINK)
            adjoint[head] = mm(
                jnp.concatenate([held[g][4], -bys[g][:, :width]], 0),
                jnp.concatenate([grad_ref[:, cols].astype(F32), reach_ref[head]], 0),
                ta=True,
            ).astype(LINK)
        for i in range(begin // mine_heads, (begin + group) // mine_heads):
            if i < len(others):
                for kind in kinds:
                    spread(mine, others[i], *kind).start()
    for ref, dst, _, _ in kinds:
        dst[mine] = ref[block(mine)]
    for kind in kinds[:2]:
        for other in others:
            spread(other, other, *kind).wait_recv()

    for h in range(mine_heads):
        pre_t[0, h] = gt[0, h].astype(F32)
        pre_b[0, h] = gb[0, h].astype(F32)
    for j in range(1, team):
        for h in range(mine_heads):
            both = mm(gt[j, h].astype(F32), jnp.concatenate([pre_t[j - 1, h], pre_b[j - 1, h]], 1))
            pre_t[j, h] = both[:, :width]
            pre_b[j, h] = both[:, width:] + gb[j, h].astype(F32)
    for other in others:
        spread(other, other, *kinds[2]).wait_recv()
    for h in range(mine_heads):
        send_g[h] = ga[team - 1, h].astype(F32)
    for j in range(team - 2, -1, -1):
        for h in range(mine_heads):
            send_g[h] = mm(gt[j, h].astype(F32), send_g[h], ta=True) + ga[j, h].astype(F32)

    def state_copy(h):
        return pltpu.make_async_remote_copy(
            src_ref=send_s.at[h], dst_ref=in_s.at[h], send_sem=ss.at[h], recv_sem=rs.at[h],
            device_id={"seq": after}, device_id_type=mesh_id,
        )

    def cotan_copy(h):
        return pltpu.make_async_remote_copy(
            src_ref=send_g.at[h], dst_ref=in_g.at[h], send_sem=sg.at[h], recv_sem=rg.at[h],
            device_id={"seq": ahead}, device_id_type=mesh_id,
        )

    def give(member, owner, src, dst, send, recv):
        return pltpu.make_async_remote_copy(
            src_ref=src.at[member], dst_ref=dst.at[block(owner)],
            send_sem=send.at[member], recv_sem=recv.at[owner],
            device_id={"seq": base + member}, device_id_type=mesh_id,
        )

    states = (out_s, back_s, bs_s, bs_r)
    cotans = (out_g, back_g, bg_s, bg_r)

    def forward():
        for h in range(mine_heads):
            @pl.when(level == 0)
            def _():
                in_s[h] = jnp.zeros_like(in_s[h])
                send_s[h] = pre_b[team - 1, h]

            @pl.when(level > 0)
            def _():
                state_copy(h).wait_recv()
                state = in_s[h]

                @pl.when(level < levels - 1)
                def _():
                    send_s[h] = mm(pre_t[team - 1, h], state) + pre_b[team - 1, h]

            @pl.when(level < levels - 1)
            def _():
                state_copy(h).start()

        for h in range(mine_heads):
            state = in_s[h]
            out_s[0, h] = state.astype(LINK)
            for j in range(1, team):
                out_s[j, h] = (mm(pre_t[j - 1, h], state) + pre_b[j - 1, h]).astype(LINK)
        for other in others:
            give(other, mine, *states).start()

    def backward():
        for h in range(mine_heads):
            @pl.when(level == levels - 1)
            def _():
                in_g[h] = jnp.zeros_like(in_g[h])

            @pl.when(level < levels - 1)
            def _():
                cotan_copy(h).wait_recv()
                cotan = in_g[h]

                @pl.when(level > 0)
                def _():
                    send_g[h] = mm(pre_t[team - 1, h], cotan, ta=True) + send_g[h]

            @pl.when(level > 0)
            def _():
                cotan_copy(h).start()

        cotans_at = [in_g[h] for h in range(mine_heads)]
        for j in range(team - 1, -1, -1):
            for h in range(mine_heads):
                out_g[j, h] = cotans_at[h].astype(LINK)
                if j:
                    cotans_at[h] = mm(gt[j, h].astype(F32), cotans_at[h], ta=True) + ga[
                        j, h
                    ].astype(F32)

        for other in others:
            give(other, mine, *cotans).start()

    @pl.when(level < levels // 2)
    def _():
        forward()
        backward()

    @pl.when(level >= levels // 2)
    def _():
        backward()
        forward()

    back_s[block(mine)] = out_s[mine]
    back_g[block(mine)] = out_g[mine]
    for other in others:
        give(mine, other, *states).wait_recv()
    for other in others:
        give(mine, other, *cotans).wait_recv()
    state_ref[...] = back_s[...].astype(F32)
    cotan_ref[...] = back_g[...].astype(F32)
    for other in others:
        for kind in kinds:
            spread(mine, other, *kind).wait_send()
        give(other, mine, *states).wait_send()
        give(other, mine, *cotans).wait_send()
    for h in range(mine_heads):
        @pl.when(level < levels - 1)
        def _():
            state_copy(h).wait_send()

        @pl.when(level > 0)
        def _():
            cotan_copy(h).wait_send()

    @pl.when(me < n - 1)
    def _():
        for j, ref in enumerate((q_ref, k_ref, v_ref)):
            halo_copy(j, ref).wait_send()


def grads_kernel(
    group,
    q_ref, k_ref, v_ref, halo_ref, gate_ref, beta_ref, w_ref, dlog_ref, grad_ref,
    inv_ref, raw_ref, att_ref, reach_ref, state_ref, cotan_ref,
    dq_ref, dk_ref, dv_ref, dgate_ref, dbeta_ref, red_ref, tail_ref, last_ref,
    ext, dext,
):
    size = q_ref.shape[0]
    half = size // 2
    width = state_ref.shape[1]
    taps = w_ref.shape[1]
    r, c = iotas(size)
    same_half = (r < half) == (c < half)
    for g in range(group):
        cols = slice(g * width, (g + 1) * width)
        head = pl.program_id(0) * group + g
        pres, rows = [], []
        for j, ref in enumerate((q_ref, k_ref, v_ref)):
            pre, row = conv_pre(ext.at[3 * g + j], ref, halo_ref, w_ref, j, cols)
            pres.append(pre)
            rows.append(row)
        sig = [sigmoid(pre) for pre in pres]
        q, q_r = unit(pres[0] * sig[0])
        k, k_r = unit(pres[1] * sig[1])
        v = pres[2] * sig[2]
        beta = sigmoid(pick_column(beta_ref, head))
        gate = gate_ref[:, cols]
        ld, speed, up, down, cross, full, end, dend, first = decays(gate, dlog_ref[:, cols])
        inv, raw, att, reach = inv_ref[g], raw_ref[g], att_ref[g], reach_ref[g]
        state, cotan = state_ref[g], cotan_ref[g]
        grad = grad_ref[:, cols].astype(F32)

        resid = v - mm(k * full, state)
        deltas = mm(inv, beta * resid)
        d_deltas = reach + mm(k * end, cotan)
        d_err = mm(inv, d_deltas, ta=True)
        d_v = beta * d_err
        stacked = jnp.concatenate([grad, -d_v], 0)
        to_full = mm(stacked, state, tb=True)
        d_qf, d_kf = to_full[:size], to_full[size:]
        scores = mm(jnp.concatenate([grad, -d_err], 0), deltas, tb=True)
        d_att = jnp.where(r >= c, scores[:size], 0.0)
        d_coup = jnp.where(r > c, scores[size:], 0.0)
        d_ke = mm(deltas, cotan, tb=True)
        d_beta = jnp.sum(d_err * resid, axis=1, keepdims=True) + jnp.sum(
            d_coup * raw, axis=1, keepdims=True
        )
        d_raw = d_coup * beta
        kc = k * cross
        both = jnp.concatenate([d_att, d_raw], 0)
        same2 = jnp.concatenate([same_half, same_half], 0)
        d_same = jnp.where(same2, both, 0.0)
        d_other = jnp.where(same2, 0.0, both)
        from_same = mm(d_same, k * down)
        from_other = mm(d_other, kc)
        to_down = mm(d_same, jnp.concatenate([q * up, k * up], 0), ta=True)
        to_cross = mm(d_other, jnp.concatenate([q * cross, kc], 0), ta=True)
        d_q = from_same[:size] * up + from_other[:size] * cross + d_qf * full
        d_k_up = from_same[size:] * up + from_other[size:] * cross + d_kf * full
        k_end_part = d_ke * end
        d_k_down = to_down * down + to_cross * cross + k_end_part
        d_k = d_k_up + d_k_down
        d_cum = q * d_q + k * (d_k_up - d_k_down)
        ones_row = jnp.ones((8, width), F32)
        end_state = mm(ones_row, state * cotan, tb=True)[0:1, :]
        d_last = jnp.sum(k * k_end_part, axis=0, keepdims=True) + dend * end_state
        d_ld = ones_mm(jnp.where(c >= r, 1.0, 0.0), d_cum) + d_last
        dgate_ref[:, cols] = speed * sigmoid(gate) * d_ld
        d_dlog = jnp.sum(ld * d_ld, axis=0, keepdims=True)
        d_braw = d_beta * beta * (1.0 - beta)
        lane = lax.broadcasted_iota(jnp.int32, dbeta_ref.shape, 1)
        dbeta_ref[...] = jnp.where(lane == head, d_braw, dbeta_ref[...])

        d_q = q_r * (d_q - q * jnp.sum(q * d_q, axis=1, keepdims=True))
        d_k = k_r * (d_k - k * jnp.sum(k * d_k, axis=1, keepdims=True))
        red = []
        for j, (d_act, out_ref) in enumerate(((d_q, dq_ref), (d_k, dk_ref), (d_v, dv_ref))):
            s = sig[j]
            d_pre = d_act * (s * (1.0 + pres[j] * (1.0 - s)))
            spot = dext.at[3 * g + j]
            spot[0:PAD, :] = jnp.zeros((PAD, width), F32)
            spot[PAD : PAD + size, :] = d_pre
            spot[PAD + size :, :] = jnp.zeros((PAD, width), F32)
            whole = None
            tail = None
            for i in range(taps):
                w = w_ref[j, i : i + 1, cols]
                start = PAD + taps - 1 - i
                term = w * spot[start : start + size, :]
                edge = w * spot[taps - 1 - i : taps - 1 - i + PAD, :]
                whole = term if whole is None else whole + term
                tail = edge if tail is None else tail + edge
                red.append(jnp.sum(d_pre * rows[j][i], axis=0, keepdims=True))
            out_ref[:, cols] = whole.astype(BF16)
            tail_ref[j, :, cols] = tail
            last_ref[j, :, cols] = whole[size - PAD :, :]
        red.append(d_dlog)
        red.append(jnp.zeros((RED - len(red), width), F32))
        red_ref[g * RED : (g + 1) * RED, :] = jnp.concatenate(red, 0)


def finish_kernel(
    red_ref, tail_ref, conv_ref, decay_ref, after_ref,
    parts, mine, result, tail_in, s1, r1, s2, r2, st, rt,
):
    n = lax.axis_size("seq")
    me = lax.axis_index("seq")
    owners = min(n, red_ref.shape[0] // 8)
    piece = red_ref.shape[0] // owners
    right = lax.rem(me + 1, n)
    left = lax.rem(me + n - 1, n)
    mesh_id = pl.DeviceIdType.MESH
    barrier = pltpu.get_barrier_semaphore()

    @pl.loop(1, n)
    def _(step):
        pl.semaphore_signal(
            barrier, inc=1, device_id={"seq": lax.rem(me + step, n)}, device_id_type=mesh_id
        )

    pl.semaphore_wait(barrier, n - 1)

    def rows(owner):
        return pl.ds(pl.multiple_of(owner * piece, 8), piece)

    tail_copy = pltpu.make_async_remote_copy(
        src_ref=tail_ref, dst_ref=tail_in, send_sem=st, recv_sem=rt,
        device_id={"seq": left}, device_id_type=mesh_id,
    )

    def scatter(owner, source):
        return pltpu.make_async_remote_copy(
            src_ref=red_ref.at[rows(owner)], dst_ref=parts.at[source],
            send_sem=s1.at[owner], recv_sem=r1.at[source],
            device_id={"seq": owner}, device_id_type=mesh_id,
        )

    def spread(target, owner):
        return pltpu.make_async_remote_copy(
            src_ref=mine, dst_ref=result.at[rows(owner)],
            send_sem=s2.at[target], recv_sem=r2.at[owner],
            device_id={"seq": target}, device_id_type=mesh_id,
        )

    @pl.loop(0, owners)
    def _(owner):
        @pl.when(owner != me)
        def _():
            scatter(owner, me).start()

    tail_copy.start()

    @pl.when(me < owners)
    def _():
        mine[...] = red_ref[rows(lax.rem(me, owners)), :]

        @pl.loop(0, n)
        def _(source):
            @pl.when(source != me)
            def _():
                scatter(lax.rem(me, owners), source).wait_recv()
                mine[...] += parts[source]

        @pl.loop(1, n)
        def _(step):
            spread(lax.rem(me + step, n), lax.rem(me, owners)).start()

        result[rows(lax.rem(me, owners)), :] = mine[...]

    @pl.loop(0, owners)
    def _(owner):
        @pl.when(owner != me)
        def _():
            spread(me, owner).wait_recv()

    width = result.shape[1]
    taps = conv_ref.shape[1]
    for h in range(result.shape[0] // RED):
        cols = slice(h * width, (h + 1) * width)
        for j in range(3):
            start = h * RED + j * taps
            conv_ref[j, :, cols] = result[start : start + taps, :]
        start = h * RED + 3 * taps
        decay_ref[:, cols] = result[start : start + 1, :]
    tail_copy.wait_recv()
    after_ref[...] = jnp.where(me == n - 1, 0.0, tail_in[...])

    @pl.loop(0, owners)
    def _(owner):
        @pl.when(owner != me)
        def _():
            scatter(owner, me).wait_send()

    @pl.when(me < owners)
    def _():
        @pl.loop(1, n)
        def _(step):
            spread(lax.rem(me + step, n), lax.rem(me, owners)).wait_send()

    tail_copy.wait_send()


def per_device(query_raw, key_raw, value_raw, gate_raw, beta_raw, conv_weight, decay_log, grad_out):
    n = lax.axis_size("seq")
    size, channels = gate_raw.shape
    heads = beta_raw.shape[1]
    width = channels // heads
    group = GROUP if heads % GROUP == 0 else 1
    steps = heads // group
    span = group * width
    dlog = decay_log.reshape(1, channels)
    vmem = pl.BlockSpec(memory_space=pltpu.VMEM)
    tokens = pl.BlockSpec((size, span), lambda h: (0, h))
    rows8 = pl.BlockSpec((3, PAD, span), lambda h: (0, 0, h))
    betas = pl.BlockSpec((size, heads), lambda h: (0, 0))
    weights = pl.BlockSpec((3, conv_weight.shape[1], span), lambda h: (0, 0, h))
    single = pl.BlockSpec((1, span), lambda h: (0, h))
    square = pl.BlockSpec((group, width, width), lambda h: (h, 0, 0))
    pairs = pl.BlockSpec((group, size, size), lambda h: (h, 0, 0))
    tall = pl.BlockSpec((group, size, width), lambda h: (h, 0, 0))
    sq = jax.ShapeDtypeStruct((heads, width, width), F32)
    pr = jax.ShapeDtypeStruct((heads, size, size), F32)
    tl = jax.ShapeDtypeStruct((heads, size, width), F32)
    params = pltpu.CompilerParams(vmem_limit_bytes=VMEM_LIMIT)
    team = math.gcd(TEAM, math.gcd(n, heads))
    part = heads // team
    block = GROUP_MAPS if heads % GROUP_MAPS == 0 and GROUP_MAPS % part == 0 else heads
    whole = pltpu.VMEM((heads, width, width), LINK)
    few = pltpu.VMEM((part, width, width), F32)
    many = pltpu.VMEM((team, part, width, width), LINK)
    wide = pltpu.VMEM((team, part, width, width), F32)
    sems = pltpu.SemaphoreType.DMA((team,))
    hops = pltpu.SemaphoreType.DMA((part,))
    three = pltpu.SemaphoreType.DMA((3,))
    head_args = (query_raw, key_raw, value_raw)
    tail_args = (gate_raw, beta_raw, conv_weight, dlog, grad_out)
    halo, inv, raw, att, reach, state, cotan = pl.pallas_call(
        functools.partial(scan_kernel, block),
        out_shape=(
            jax.ShapeDtypeStruct((3, PAD, channels), query_raw.dtype), pr, pr, pr, tl, sq, sq,
        ),
        in_specs=[vmem] * 8,
        out_specs=(vmem,) * 7,
        scratch_shapes=[
            pltpu.VMEM((3 * block, PAD + size, width), F32),
            pltpu.VMEM((3, PAD, channels), query_raw.dtype),
        ]
        + [whole] * 3 + [many] * 3 + [wide] * 2 + [few] * 4 + [many] * 2 + [whole] * 2
        + [three] * 2 + [sems] * 6 + [hops] * 4 + [sems] * 4,
        compiler_params=pltpu.CompilerParams(
            collective_id=0, has_side_effects=True, vmem_limit_bytes=VMEM_LIMIT
        ),
        name="scan",
    )(*head_args, *tail_args)
    common = head_args + (halo,) + tail_args
    common_specs = [
        tokens, tokens, tokens, rows8, tokens, betas, weights, single, tokens,
    ]

    act = jax.ShapeDtypeStruct((size, channels), BF16)
    edge = jax.ShapeDtypeStruct((3, PAD, channels), F32)
    dq, dk, dv, dgate, dbeta, red, tail, last = pl.pallas_call(
        functools.partial(grads_kernel, group),
        grid=(steps,),
        out_shape=(
            act, act, act,
            jax.ShapeDtypeStruct((size, channels), F32),
            jax.ShapeDtypeStruct((size, heads), F32),
            jax.ShapeDtypeStruct((heads * RED, width), F32),
            edge, edge,
        ),
        in_specs=common_specs + [pairs, pairs, pairs, tall, square, square],
        out_specs=(
            tokens, tokens, tokens, tokens, betas,
            pl.BlockSpec((group * RED, width), lambda h: (h, 0)),
            rows8, rows8,
        ),
        scratch_shapes=[
            pltpu.VMEM((3 * group, PAD + size, width), F32),
            pltpu.VMEM((3 * group, PAD + size + PAD, width), F32),
        ],
        compiler_params=params,
        name="grads",
    )(*common, inv, raw, att, reach, state, cotan)

    owners = min(n, heads * RED // 8)
    piece = heads * RED // owners
    conv_sum, decay_sum, after = pl.pallas_call(
        finish_kernel,
        out_shape=(
            jax.ShapeDtypeStruct(conv_weight.shape, F32),
            jax.ShapeDtypeStruct((1, channels), F32),
            edge,
        ),
        in_specs=[vmem] * 2,
        out_specs=(vmem, vmem, vmem),
        scratch_shapes=[
            pltpu.VMEM((n, piece, width), F32),
            pltpu.VMEM((piece, width), F32),
            pltpu.VMEM(red.shape, F32),
            pltpu.VMEM(edge.shape, F32),
            pltpu.SemaphoreType.DMA((owners,)),
            pltpu.SemaphoreType.DMA((n,)),
            pltpu.SemaphoreType.DMA((n,)),
            pltpu.SemaphoreType.DMA((owners,)),
            pltpu.SemaphoreType.DMA,
            pltpu.SemaphoreType.DMA,
        ],
        compiler_params=pltpu.CompilerParams(
            collective_id=1, has_side_effects=True, vmem_limit_bytes=VMEM_LIMIT
        ),
        name="finish",
    )(red, tail)

    ends = (last + after).astype(BF16)
    dq = lax.dynamic_update_slice(dq, ends[0], (size - PAD, 0))
    dk = lax.dynamic_update_slice(dk, ends[1], (size - PAD, 0))
    dv = lax.dynamic_update_slice(dv, ends[2], (size - PAD, 0))
    return (dq, dk, dv, dgate, dbeta, conv_sum, decay_sum.reshape(channels))


def solution(mesh):
    in_specs = (
        P("seq", "head"),
        P("seq", "head"),
        P("seq", "head"),
        P("seq", "head"),
        P("seq", "head"),
        P(None, None, "head"),
        P("head"),
        P("seq", "head"),
    )
    out_specs = (
        P("seq", "head"),
        P("seq", "head"),
        P("seq", "head"),
        P("seq", "head"),
        P("seq", "head"),
        P(None, None, "head"),
        P("head"),
    )
    return jax.shard_map(
        per_device, mesh=mesh, in_specs=in_specs, out_specs=out_specs, check_vma=False
    )
```

```python
import functools
import math

import jax
import jax.numpy as jnp
from jax import lax
from jax.experimental import pallas as pl
from jax.experimental.pallas import tpu as pltpu
from jax.sharding import PartitionSpec as P

F32 = jnp.float32
BF16 = jnp.bfloat16
EPS = 1e-06
PAD = 8
RED = 16
GROUP = 4
GROUP_MAPS = 4
LINK = F32
TEAM = 4
VMEM_LIMIT = 60 * 1024 * 1024


def split(x):
    hi = x.astype(BF16)
    return hi, (x - hi.astype(F32)).astype(BF16)


def mm(a, b, ta=False, tb=False):
    ah, al = split(a)
    bh, bl = split(b)
    lhs = jnp.concatenate([ah, al], 0 if ta else 1)
    if tb:
        rhs = jnp.concatenate(
            [jnp.concatenate([bh, bh], 1), jnp.concatenate([bl, bl], 1)], 0
        )
    else:
        row = jnp.concatenate([bh, bl], 1)
        rhs = jnp.concatenate([row, row], 0)
    out = lax.dot_general(
        lhs,
        rhs,
        (((0 if ta else 1,), (1 if tb else 0,)), ((), ())),
        preferred_element_type=F32,
    )
    n = out.shape[1] // 2
    return out[:, :n] + out[:, n:]


def ones_mm(ones, x):
    hi, mid = split(x)
    low = (x - hi.astype(F32) - mid.astype(F32)).astype(BF16)
    n = x.shape[1]
    out = jnp.dot(
        ones.astype(BF16), jnp.concatenate([hi, mid, low], 1), preferred_element_type=F32
    )
    return out[:, :n] + out[:, n : 2 * n] + out[:, 2 * n :]


def sigmoid(x):
    return 1.0 / (1.0 + jnp.exp(-x))


def softplus(x):
    return jnp.maximum(x, 0.0) + jnp.log1p(jnp.exp(-jnp.abs(x)))


def iotas(size):
    r = lax.broadcasted_iota(jnp.int32, (size, size), 0)
    c = lax.broadcasted_iota(jnp.int32, (size, size), 1)
    return r, c


def conv_pre(ext, x_ref, halo_ref, w_ref, j, cols):
    size = x_ref.shape[0]
    ext[0:PAD, :] = halo_ref[j, :, cols].astype(F32)
    ext[PAD : PAD + size, :] = x_ref[:, cols].astype(F32)
    taps = w_ref.shape[1]
    rows = [ext[PAD - taps + 1 + i : PAD - taps + 1 + i + size, :] for i in range(taps)]
    pre = w_ref[j, 0:1, cols] * rows[0]
    for i in range(1, taps):
        pre = pre + w_ref[j, i : i + 1, cols] * rows[i]
    return pre, rows


def pick_column(ref, index):
    row = ref[pl.ds(index, 1), :]
    r, c = iotas(row.shape[1])
    return jnp.sum(jnp.where(r == c, row, 0.0), axis=1, keepdims=True)


def unit(x):
    r = lax.rsqrt(jnp.sum(x * x, axis=1, keepdims=True) + EPS)
    return x * r, r


def decays(gate, dlog):
    size = gate.shape[0]
    half = size // 2
    r, c = iotas(size)
    speed = -jnp.exp(dlog)
    ld = speed * softplus(gate)
    cum = ones_mm(jnp.where(r >= c, 1.0, 0.0), ld)
    row = lax.broadcasted_iota(jnp.int32, gate.shape, 0)
    first = row < half
    mid = jnp.where(
        first, cum[half // 2 : half // 2 + 1, :], cum[half + half // 2 : half + half // 2 + 1, :]
    )
    edge = cum[half - 1 : half, :]
    last = cum[size - 1 : size, :]
    up = jnp.exp(cum - mid)
    down = jnp.exp(mid - cum)
    cross = jnp.exp(jnp.where(first, edge - cum, cum - edge))
    full = jnp.exp(cum)
    end = jnp.exp(last - cum)
    return ld, speed, up, down, cross, full, end, jnp.exp(last), first


def pair_scores(qk_up, k_down, qk_cross, k_cross):
    size = k_down.shape[0]
    half = size // 2
    same = mm(qk_up, k_down, tb=True)
    other = mm(qk_cross, k_cross, tb=True)
    r, c = iotas(size)
    same_half = (r < half) == (c < half)
    return (
        jnp.where(same_half, same[:size], other[:size]),
        jnp.where(same_half, same[size:], other[size:]),
    )


def unit_inverses(coups):
    size = coups[0].shape[0]
    r, c = iotas(size)
    ident = jnp.where(r == c, 1.0, 0.0)
    shift = 3
    inside = (r >> shift) == (c >> shift)
    small = [jnp.where(inside, a, 0.0) for a in coups]
    p2 = [mm(a, a) for a in small]
    base = [ident - a for a in small]
    p4 = [mm(p, p) for p in p2]
    base = [x + mm(x, p) for x, p in zip(base, p2)]
    d = [x + mm(x, p) for x, p in zip(base, p4)]
    while (1 << shift) < size:
        joined = ((r >> (shift + 1)) == (c >> (shift + 1))) & ((r >> shift) != (c >> shift))
        low = [mm(jnp.where(joined, a, 0.0), x) for a, x in zip(coups, d)]
        d = [x - mm(x, y) for x, y in zip(d, low)]
        shift += 1
    return d


def scan_kernel(
    group,
    q_ref, k_ref, v_ref, gate_ref, beta_ref, w_ref, dlog_ref, grad_ref,
    halo_ref, inv_ref, raw_ref, att_ref, reach_ref, state_ref, cotan_ref,
    ext, halo_in, trans, offset, adjoint,
    gt, gb, ga, pre_t, pre_b, send_s, send_g, in_s, in_g, out_s, out_g, back_s, back_g,
    hs, hr, at_s, at_r, ab_s, ab_r, aa_s, aa_r, ss, rs, sg, rg, bs_s, bs_r, bg_s, bg_r,
):
    n = lax.axis_size("seq")
    me = lax.axis_index("seq")
    team, mine_heads = gt.shape[0], gt.shape[1]
    mine = lax.rem(me, team)
    base = me - mine
    level = me // team
    levels = n // team
    mesh_id = pl.DeviceIdType.MESH
    right = lax.rem(me + 1, n)
    left = lax.rem(me + n - 1, n)
    after = lax.rem(me + team, n)
    ahead = lax.rem(me + n - team, n)
    barrier = pltpu.get_barrier_semaphore()
    peers = [base + lax.rem(mine + i, team) for i in range(1, team)]
    links = peers + [right, left] + ([after, ahead] if levels > 1 else [])
    for peer in links:
        pl.semaphore_signal(barrier, inc=1, device_id={"seq": peer}, device_id_type=mesh_id)
    pl.semaphore_wait(barrier, len(links))

    size = q_ref.shape[0]
    heads, width = trans.shape[0], trans.shape[1]

    def halo_copy(j, ref):
        return pltpu.make_async_remote_copy(
            src_ref=ref.at[pl.ds(size - PAD, PAD)], dst_ref=halo_in.at[j],
            send_sem=hs.at[j], recv_sem=hr.at[j],
            device_id={"seq": right}, device_id_type=mesh_id,
        )

    @pl.when(me < n - 1)
    def _():
        for j, ref in enumerate((q_ref, k_ref, v_ref)):
            halo_copy(j, ref).start()

    def block(member):
        return pl.ds(member * mine_heads, mine_heads)

    def spread(source, target, ref, dst, send, recv):
        return pltpu.make_async_remote_copy(
            src_ref=ref.at[block(target)], dst_ref=dst.at[source],
            send_sem=send.at[target], recv_sem=recv.at[source],
            device_id={"seq": base + target}, device_id_type=mesh_id,
        )

    kinds = (
        (trans, gt, at_s, at_r), (offset, gb, ab_s, ab_r), (adjoint, ga, aa_s, aa_r)
    )
    others = [lax.rem(mine + i, team) for i in range(1, team)]
    order = others + [mine]
    r, c = iotas(size)
    rr, cc = iotas(width)
    for begin in range(0, heads, group):
        held = []
        places = []
        for g in range(group):
            at = begin + g
            head = order[at // mine_heads] * mine_heads + at % mine_heads
            places.append((head, pl.ds(pl.multiple_of(head * width, width), width)))
        fades = [decays(gate_ref[:, cols], dlog_ref[:, cols]) for _, cols in places]
        if begin == 0:
            @pl.when(me == 0)
            def _():
                halo_in[...] = jnp.zeros_like(halo_in)

            @pl.when(me > 0)
            def _():
                for j, ref in enumerate((q_ref, k_ref, v_ref)):
                    halo_copy(j, ref).wait_recv()

            halo_ref[...] = halo_in[...]
        for g, (head, cols) in enumerate(places):
            pre_q, _ = conv_pre(ext.at[3 * g], q_ref, halo_in, w_ref, 0, cols)
            pre_k, _ = conv_pre(ext.at[3 * g + 1], k_ref, halo_in, w_ref, 1, cols)
            pre_v, _ = conv_pre(ext.at[3 * g + 2], v_ref, halo_in, w_ref, 2, cols)
            q, _ = unit(pre_q * sigmoid(pre_q))
            k, _ = unit(pre_k * sigmoid(pre_k))
            v = pre_v * sigmoid(pre_v)
            beta = sigmoid(pick_column(beta_ref, head))
            ld, speed, up, down, cross, full, end, dend, first = fades[g]
            kc = k * cross
            qk_up = jnp.concatenate([q * up, k * up], 0)
            qk_cross = jnp.concatenate([q * cross, kc], 0)
            att, raw = pair_scores(qk_up, k * down, qk_cross, kc)
            att = jnp.where(r >= c, att, 0.0)
            raw = jnp.where(r > c, raw, 0.0)
            raw_ref[head] = raw
            att_ref[head] = att
            reach_ref[head] = mm(att, grad_ref[:, cols].astype(F32), ta=True)
            inputs = jnp.concatenate([beta * k * full, beta * v], 1)
            held.append((raw * beta, inputs, k * end, dend, q * full))
        invs = unit_inverses([item[0] for item in held])
        bys = [mm(inv, item[1]) for inv, item in zip(invs, held)]
        for g, (head, cols) in enumerate(places):
            inv_ref[head] = invs[g]
            ends = mm(held[g][2], bys[g], ta=True)
            trans[head] = (jnp.where(rr == cc, held[g][3], 0.0) - ends[:, :width]).astype(LINK)
            offset[head] = ends[:, width:].astype(LINK)
            adjoint[head] = mm(
                jnp.concatenate([held[g][4], -bys[g][:, :width]], 0),
                jnp.concatenate([grad_ref[:, cols].astype(F32), reach_ref[head]], 0),
                ta=True,
            ).astype(LINK)
        for i in range(begin // mine_heads, (begin + group) // mine_heads):
            if i < len(others):
                for kind in kinds:
                    spread(mine, others[i], *kind).start()
    for ref, dst, _, _ in kinds:
        dst[mine] = ref[block(mine)]
    for kind in kinds[:2]:
        for other in others:
            spread(other, other, *kind).wait_recv()

    for h in range(mine_heads):
        pre_t[0, h] = gt[0, h].astype(F32)
        pre_b[0, h] = gb[0, h].astype(F32)
    for j in range(1, team):
        for h in range(mine_heads):
            both = mm(gt[j, h].astype(F32), jnp.concatenate([pre_t[j - 1, h], pre_b[j - 1, h]], 1))
            pre_t[j, h] = both[:, :width]
            pre_b[j, h] = both[:, width:] + gb[j, h].astype(F32)
    for other in others:
        spread(other, other, *kinds[2]).wait_recv()
    for h in range(mine_heads):
        send_g[h] = ga[team - 1, h].astype(F32)
    for j in range(team - 2, -1, -1):
        for h in range(mine_heads):
            send_g[h] = mm(gt[j, h].astype(F32), send_g[h], ta=True) + ga[j, h].astype(F32)

    def state_copy(h):
        return pltpu.make_async_remote_copy(
            src_ref=send_s.at[h], dst_ref=in_s.at[h], send_sem=ss.at[h], recv_sem=rs.at[h],
            device_id={"seq": after}, device_id_type=mesh_id,
        )

    def cotan_copy(h):
        return pltpu.make_async_remote_copy(
            src_ref=send_g.at[h], dst_ref=in_g.at[h], send_sem=sg.at[h], recv_sem=rg.at[h],
            device_id={"seq": ahead}, device_id_type=mesh_id,
        )

    def give(member, owner, src, dst, send, recv):
        return pltpu.make_async_remote_copy(
            src_ref=src.at[member], dst_ref=dst.at[block(owner)],
            send_sem=send.at[member], recv_sem=recv.at[owner],
            device_id={"seq": base + member}, device_id_type=mesh_id,
        )

    states = (out_s, back_s, bs_s, bs_r)
    cotans = (out_g, back_g, bg_s, bg_r)

    def forward():
        for h in range(mine_heads):
            @pl.when(level == 0)
            def _():
                in_s[h] = jnp.zeros_like(in_s[h])
                send_s[h] = pre_b[team - 1, h]

            @pl.when(level > 0)
            def _():
                state_copy(h).wait_recv()
                state = in_s[h]

                @pl.when(level < levels - 1)
                def _():
                    send_s[h] = mm(pre_t[team - 1, h], state) + pre_b[team - 1, h]

            @pl.when(level < levels - 1)
            def _():
                state_copy(h).start()

        for h in range(mine_heads):
            state = in_s[h]
            out_s[0, h] = state.astype(LINK)
            for j in range(1, team):
                out_s[j, h] = (mm(pre_t[j - 1, h], state) + pre_b[j - 1, h]).astype(LINK)
        for other in others:
            give(other, mine, *states).start()

    def backward():
        for h in range(mine_heads):
            @pl.when(level == levels - 1)
            def _():
                in_g[h] = jnp.zeros_like(in_g[h])

            @pl.when(level < levels - 1)
            def _():
                cotan_copy(h).wait_recv()
                cotan = in_g[h]

                @pl.when(level > 0)
                def _():
                    send_g[h] = mm(pre_t[team - 1, h], cotan, ta=True) + send_g[h]

            @pl.when(level > 0)
            def _():
                cotan_copy(h).start()

        cotans_at = [in_g[h] for h in range(mine_heads)]
        for j in range(team - 1, -1, -1):
            for h in range(mine_heads):
                out_g[j, h] = cotans_at[h].astype(LINK)
                if j:
                    cotans_at[h] = mm(gt[j, h].astype(F32), cotans_at[h], ta=True) + ga[
                        j, h
                    ].astype(F32)

        for other in others:
            give(other, mine, *cotans).start()

    @pl.when(level < levels // 2)
    def _():
        forward()
        backward()

    @pl.when(level >= levels // 2)
    def _():
        backward()
        forward()

    back_s[block(mine)] = out_s[mine]
    back_g[block(mine)] = out_g[mine]
    for other in others:
        give(mine, other, *states).wait_recv()
    for other in others:
        give(mine, other, *cotans).wait_recv()
    state_ref[...] = back_s[...].astype(F32)
    cotan_ref[...] = back_g[...].astype(F32)
    for other in others:
        for kind in kinds:
            spread(mine, other, *kind).wait_send()
        give(other, mine, *states).wait_send()
        give(other, mine, *cotans).wait_send()
    for h in range(mine_heads):
        @pl.when(level < levels - 1)
        def _():
            state_copy(h).wait_send()

        @pl.when(level > 0)
        def _():
            cotan_copy(h).wait_send()

    @pl.when(me < n - 1)
    def _():
        for j, ref in enumerate((q_ref, k_ref, v_ref)):
            halo_copy(j, ref).wait_send()


def grads_kernel(
    group,
    q_ref, k_ref, v_ref, halo_ref, gate_ref, beta_ref, w_ref, dlog_ref, grad_ref,
    inv_ref, raw_ref, att_ref, reach_ref, state_ref, cotan_ref,
    dq_ref, dk_ref, dv_ref, dgate_ref, dbeta_ref, red_ref, tail_ref, last_ref,
    ext, dext,
):
    size = q_ref.shape[0]
    half = size // 2
    width = state_ref.shape[1]
    taps = w_ref.shape[1]
    r, c = iotas(size)
    same_half = (r < half) == (c < half)
    for g in range(group):
        cols = slice(g * width, (g + 1) * width)
        head = pl.program_id(0) * group + g
        pres, rows = [], []
        for j, ref in enumerate((q_ref, k_ref, v_ref)):
            pre, row = conv_pre(ext.at[3 * g + j], ref, halo_ref, w_ref, j, cols)
            pres.append(pre)
            rows.append(row)
        sig = [sigmoid(pre) for pre in pres]
        q, q_r = unit(pres[0] * sig[0])
        k, k_r = unit(pres[1] * sig[1])
        v = pres[2] * sig[2]
        beta = sigmoid(pick_column(beta_ref, head))
        gate = gate_ref[:, cols]
        ld, speed, up, down, cross, full, end, dend, first = decays(gate, dlog_ref[:, cols])
        inv, raw, att, reach = inv_ref[g], raw_ref[g], att_ref[g], reach_ref[g]
        state, cotan = state_ref[g], cotan_ref[g]
        grad = grad_ref[:, cols].astype(F32)

        resid = v - mm(k * full, state)
        deltas = mm(inv, beta * resid)
        d_deltas = reach + mm(k * end, cotan)
        d_err = mm(inv, d_deltas, ta=True)
        d_v = beta * d_err
        stacked = jnp.concatenate([grad, -d_v], 0)
        to_full = mm(stacked, state, tb=True)
        d_qf, d_kf = to_full[:size], to_full[size:]
        scores = mm(jnp.concatenate([grad, -d_err], 0), deltas, tb=True)
        d_att = jnp.where(r >= c, scores[:size], 0.0)
        d_coup = jnp.where(r > c, scores[size:], 0.0)
        d_ke = mm(deltas, cotan, tb=True)
        d_beta = jnp.sum(d_err * resid, axis=1, keepdims=True) + jnp.sum(
            d_coup * raw, axis=1, keepdims=True
        )
        d_raw = d_coup * beta
        kc = k * cross
        both = jnp.concatenate([d_att, d_raw], 0)
        same2 = jnp.concatenate([same_half, same_half], 0)
        d_same = jnp.where(same2, both, 0.0)
        d_other = jnp.where(same2, 0.0, both)
        from_same = mm(d_same, k * down)
        from_other = mm(d_other, kc)
        to_down = mm(d_same, jnp.concatenate([q * up, k * up], 0), ta=True)
        to_cross = mm(d_other, jnp.concatenate([q * cross, kc], 0), ta=True)
        d_q = from_same[:size] * up + from_other[:size] * cross + d_qf * full
        d_k_up = from_same[size:] * up + from_other[size:] * cross + d_kf * full
        k_end_part = d_ke * end
        d_k_down = to_down * down + to_cross * cross + k_end_part
        d_k = d_k_up + d_k_down
        d_cum = q * d_q + k * (d_k_up - d_k_down)
        ones_row = jnp.ones((8, width), F32)
        end_state = mm(ones_row, state * cotan, tb=True)[0:1, :]
        d_last = jnp.sum(k * k_end_part, axis=0, keepdims=True) + dend * end_state
        d_ld = ones_mm(jnp.where(c >= r, 1.0, 0.0), d_cum) + d_last
        dgate_ref[:, cols] = speed * sigmoid(gate) * d_ld
        d_dlog = jnp.sum(ld * d_ld, axis=0, keepdims=True)
        d_braw = d_beta * beta * (1.0 - beta)
        dbeta_ref[pl.ds(head, 1), :] = jnp.sum(
            jnp.where(r == c, d_braw, 0.0), axis=0, keepdims=True
        )

        d_q = q_r * (d_q - q * jnp.sum(q * d_q, axis=1, keepdims=True))
        d_k = k_r * (d_k - k * jnp.sum(k * d_k, axis=1, keepdims=True))
        red = []
        for j, (d_act, out_ref) in enumerate(((d_q, dq_ref), (d_k, dk_ref), (d_v, dv_ref))):
            s = sig[j]
            d_pre = d_act * (s * (1.0 + pres[j] * (1.0 - s)))
            spot = dext.at[3 * g + j]
            spot[0:PAD, :] = jnp.zeros((PAD, width), F32)
            spot[PAD : PAD + size, :] = d_pre
            spot[PAD + size :, :] = jnp.zeros((PAD, width), F32)
            whole = None
            tail = None
            for i in range(taps):
                w = w_ref[j, i : i + 1, cols]
                start = PAD + taps - 1 - i
                term = w * spot[start : start + size, :]
                edge = w * spot[taps - 1 - i : taps - 1 - i + PAD, :]
                whole = term if whole is None else whole + term
                tail = edge if tail is None else tail + edge
                red.append(jnp.sum(d_pre * rows[j][i], axis=0, keepdims=True))
            out_ref[:, cols] = whole.astype(BF16)
            tail_ref[j, :, cols] = tail
            last_ref[j, :, cols] = whole[size - PAD :, :]
        red.append(d_dlog)
        red.append(jnp.zeros((RED - len(red), width), F32))
        red_ref[g * RED : (g + 1) * RED, :] = jnp.concatenate(red, 0)


def finish_kernel(
    red_ref, tail_ref, conv_ref, decay_ref, after_ref,
    parts, mine, result, tail_in, s1, r1, s2, r2, st, rt,
):
    n = lax.axis_size("seq")
    me = lax.axis_index("seq")
    owners = min(n, red_ref.shape[0] // 8)
    piece = red_ref.shape[0] // owners
    right = lax.rem(me + 1, n)
    left = lax.rem(me + n - 1, n)
    mesh_id = pl.DeviceIdType.MESH
    barrier = pltpu.get_barrier_semaphore()

    @pl.loop(1, n)
    def _(step):
        pl.semaphore_signal(
            barrier, inc=1, device_id={"seq": lax.rem(me + step, n)}, device_id_type=mesh_id
        )

    pl.semaphore_wait(barrier, n - 1)

    def rows(owner):
        return pl.ds(pl.multiple_of(owner * piece, 8), piece)

    tail_copy = pltpu.make_async_remote_copy(
        src_ref=tail_ref, dst_ref=tail_in, send_sem=st, recv_sem=rt,
        device_id={"seq": left}, device_id_type=mesh_id,
    )

    def scatter(owner, source):
        return pltpu.make_async_remote_copy(
            src_ref=red_ref.at[rows(owner)], dst_ref=parts.at[source],
            send_sem=s1.at[owner], recv_sem=r1.at[source],
            device_id={"seq": owner}, device_id_type=mesh_id,
        )

    def spread(target, owner):
        return pltpu.make_async_remote_copy(
            src_ref=mine, dst_ref=result.at[rows(owner)],
            send_sem=s2.at[target], recv_sem=r2.at[owner],
            device_id={"seq": target}, device_id_type=mesh_id,
        )

    @pl.loop(0, owners)
    def _(owner):
        @pl.when(owner != me)
        def _():
            scatter(owner, me).start()

    tail_copy.start()

    @pl.when(me < owners)
    def _():
        mine[...] = red_ref[rows(lax.rem(me, owners)), :]

        @pl.loop(0, n)
        def _(source):
            @pl.when(source != me)
            def _():
                scatter(lax.rem(me, owners), source).wait_recv()
                mine[...] += parts[source]

        @pl.loop(1, n)
        def _(step):
            spread(lax.rem(me + step, n), lax.rem(me, owners)).start()

        result[rows(lax.rem(me, owners)), :] = mine[...]

    @pl.loop(0, owners)
    def _(owner):
        @pl.when(owner != me)
        def _():
            spread(me, owner).wait_recv()

    width = result.shape[1]
    taps = conv_ref.shape[1]
    for h in range(result.shape[0] // RED):
        cols = slice(h * width, (h + 1) * width)
        for j in range(3):
            start = h * RED + j * taps
            conv_ref[j, :, cols] = result[start : start + taps, :]
        start = h * RED + 3 * taps
        decay_ref[:, cols] = result[start : start + 1, :]
    tail_copy.wait_recv()
    after_ref[...] = jnp.where(me == n - 1, 0.0, tail_in[...])

    @pl.loop(0, owners)
    def _(owner):
        @pl.when(owner != me)
        def _():
            scatter(owner, me).wait_send()

    @pl.when(me < owners)
    def _():
        @pl.loop(1, n)
        def _(step):
            spread(lax.rem(me + step, n), lax.rem(me, owners)).wait_send()

    tail_copy.wait_send()


def per_device(query_raw, key_raw, value_raw, gate_raw, beta_raw, conv_weight, decay_log, grad_out):
    n = lax.axis_size("seq")
    size, channels = gate_raw.shape
    heads = beta_raw.shape[1]
    width = channels // heads
    group = GROUP if heads % GROUP == 0 else 1
    steps = heads // group
    span = group * width
    dlog = decay_log.reshape(1, channels)
    vmem = pl.BlockSpec(memory_space=pltpu.VMEM)
    tokens = pl.BlockSpec((size, span), lambda h: (0, h))
    rows8 = pl.BlockSpec((3, PAD, span), lambda h: (0, 0, h))
    betas = pl.BlockSpec((heads, size), lambda h: (0, 0))
    weights = pl.BlockSpec((3, conv_weight.shape[1], span), lambda h: (0, 0, h))
    single = pl.BlockSpec((1, span), lambda h: (0, h))
    square = pl.BlockSpec((group, width, width), lambda h: (h, 0, 0))
    pairs = pl.BlockSpec((group, size, size), lambda h: (h, 0, 0))
    tall = pl.BlockSpec((group, size, width), lambda h: (h, 0, 0))
    sq = jax.ShapeDtypeStruct((heads, width, width), F32)
    pr = jax.ShapeDtypeStruct((heads, size, size), F32)
    tl = jax.ShapeDtypeStruct((heads, size, width), F32)
    params = pltpu.CompilerParams(vmem_limit_bytes=VMEM_LIMIT)
    team = math.gcd(TEAM, math.gcd(n, heads))
    part = heads // team
    block = GROUP_MAPS if heads % GROUP_MAPS == 0 and GROUP_MAPS % part == 0 else heads
    whole = pltpu.VMEM((heads, width, width), LINK)
    few = pltpu.VMEM((part, width, width), F32)
    many = pltpu.VMEM((team, part, width, width), LINK)
    wide = pltpu.VMEM((team, part, width, width), F32)
    sems = pltpu.SemaphoreType.DMA((team,))
    hops = pltpu.SemaphoreType.DMA((part,))
    three = pltpu.SemaphoreType.DMA((3,))
    head_args = (query_raw, key_raw, value_raw)
    tail_args = (gate_raw, beta_raw.T, conv_weight, dlog, grad_out)
    halo, inv, raw, att, reach, state, cotan = pl.pallas_call(
        functools.partial(scan_kernel, block),
        out_shape=(
            jax.ShapeDtypeStruct((3, PAD, channels), query_raw.dtype), pr, pr, pr, tl, sq, sq,
        ),
        in_specs=[vmem] * 8,
        out_specs=(vmem,) * 7,
        scratch_shapes=[
            pltpu.VMEM((3 * block, PAD + size, width), F32),
            pltpu.VMEM((3, PAD, channels), query_raw.dtype),
        ]
        + [whole] * 3 + [many] * 3 + [wide] * 2 + [few] * 4 + [many] * 2 + [whole] * 2
        + [three] * 2 + [sems] * 6 + [hops] * 4 + [sems] * 4,
        compiler_params=pltpu.CompilerParams(
            collective_id=0, has_side_effects=True, vmem_limit_bytes=VMEM_LIMIT
        ),
        name="scan",
    )(*head_args, *tail_args)
    common = head_args + (halo,) + tail_args
    common_specs = [
        tokens, tokens, tokens, rows8, tokens, betas, weights, single, tokens,
    ]

    act = jax.ShapeDtypeStruct((size, channels), BF16)
    edge = jax.ShapeDtypeStruct((3, PAD, channels), F32)
    dq, dk, dv, dgate, dbeta, red, tail, last = pl.pallas_call(
        functools.partial(grads_kernel, group),
        grid=(steps,),
        out_shape=(
            act, act, act,
            jax.ShapeDtypeStruct((size, channels), F32),
            jax.ShapeDtypeStruct((heads, size), F32),
            jax.ShapeDtypeStruct((heads * RED, width), F32),
            edge, edge,
        ),
        in_specs=common_specs + [pairs, pairs, pairs, tall, square, square],
        out_specs=(
            tokens, tokens, tokens, tokens, betas,
            pl.BlockSpec((group * RED, width), lambda h: (h, 0)),
            rows8, rows8,
        ),
        scratch_shapes=[
            pltpu.VMEM((3 * group, PAD + size, width), F32),
            pltpu.VMEM((3 * group, PAD + size + PAD, width), F32),
        ],
        compiler_params=params,
        name="grads",
    )(*common, inv, raw, att, reach, state, cotan)

    owners = min(n, heads * RED // 8)
    piece = heads * RED // owners
    conv_sum, decay_sum, after = pl.pallas_call(
        finish_kernel,
        out_shape=(
            jax.ShapeDtypeStruct(conv_weight.shape, F32),
            jax.ShapeDtypeStruct((1, channels), F32),
            edge,
        ),
        in_specs=[vmem] * 2,
        out_specs=(vmem, vmem, vmem),
        scratch_shapes=[
            pltpu.VMEM((n, piece, width), F32),
            pltpu.VMEM((piece, width), F32),
            pltpu.VMEM(red.shape, F32),
            pltpu.VMEM(edge.shape, F32),
            pltpu.SemaphoreType.DMA((owners,)),
            pltpu.SemaphoreType.DMA((n,)),
            pltpu.SemaphoreType.DMA((n,)),
            pltpu.SemaphoreType.DMA((owners,)),
            pltpu.SemaphoreType.DMA,
            pltpu.SemaphoreType.DMA,
        ],
        compiler_params=pltpu.CompilerParams(
            collective_id=1, has_side_effects=True, vmem_limit_bytes=VMEM_LIMIT
        ),
        name="finish",
    )(red, tail)

    ends = (last + after).astype(BF16)
    dq = lax.dynamic_update_slice(dq, ends[0], (size - PAD, 0))
    dk = lax.dynamic_update_slice(dk, ends[1], (size - PAD, 0))
    dv = lax.dynamic_update_slice(dv, ends[2], (size - PAD, 0))
    return (dq, dk, dv, dgate, dbeta.T, conv_sum, decay_sum.reshape(channels))


def solution(mesh):
    in_specs = (
        P("seq", "head"),
        P("seq", "head"),
        P("seq", "head"),
        P("seq", "head"),
        P("seq", "head"),
        P(None, None, "head"),
        P("head"),
        P("seq", "head"),
    )
    out_specs = (
        P("seq", "head"),
        P("seq", "head"),
        P("seq", "head"),
        P("seq", "head"),
        P("seq", "head"),
        P(None, None, "head"),
        P("head"),
    )
    return jax.shard_map(
        per_device, mesh=mesh, in_specs=in_specs, out_specs=out_specs, check_vma=False
    )
```
